32 devices in a mesh: band: 4 (over y, core), mem: 8 (over z, x).
Axes of the slice: x: 2, y: 2, z: 4, core: 2. Of those that a mesh axis runs over, the one named last changes fastest.
Arguments:
- latent: bfloat16 [8, 32, 512, 512], P('mem', 'band'), may hold values from -6 to 6
- truth: float32 [80, 32, 512], P(None, 'band', 'mem'), may hold values from -6 to 6
- node_weight: float32 [32, 512], P('band', 'mem'), may hold values from 0.25 to 1
- first_weight: bfloat16 [512, 512], replicated, may hold values from -0.25 to 0.25
- first_bias: float32 [512], replicated, may hold values from -3 to 3
- second_weight: bfloat16 [512, 512], replicated, may hold values from -0.25 to 0.25
- second_bias: float32 [512], replicated, may hold values from -3 to 3
- out_weight: bfloat16 [80, 512], replicated, may hold values from -0.25 to 0.25
- out_bias: float32 [80], replicated, may hold values from -3 to 3
Outputs:
- score: float32 [32, 512], P('band', 'mem')
- grad_first_weight: float32 [512, 512], P('mem')
- grad_first_bias: float32 [512], replicated
- grad_second_weight: float32 [512, 512], P('mem')
- grad_second_bias: float32 [512], replicated
- grad_out_weight: float32 [80, 512], replicated
- grad_out_bias: float32 [80], replicated
The draws below stay inside these ranges and needn't reach their ends.
All inputs are finite; a program needn't handle non-finite values.
Results may differ from the reference program's by a relative error of at most 0.0014.
Values sent between devices are 32-bit elements; how exact they have to be, the bound alone decides.
A program may use at most 128 MiB of HBM per device.

```python
import math
import jax
import jax.numpy as jnp
from jax import lax

LATENT = 512
HIDDEN_SIZE = 512
CHANNELS = 80
RADIUS = 3
LONGITUDES = 512
MEMBERS = 8
LATITUDES = 32
CELLS = 16384
SCORE_CELLS = 512


def strengthened(result, rng, source, target, parts, factor):
    owner, partner = [(jnp.arange(result.shape[axis_at]) // (result.shape[axis_at] // parts)).reshape([-1 if axis == axis_at else 1 for axis in range(result.ndim)]) for axis_at in (source, target)]
    chosen = jax.random.permutation(rng, parts)[partner]
    strong = (owner == chosen) | (owner == (partner + parts // 2) % parts)
    return jnp.where(strong, factor * result, result)


def block_levels(stream_key, shape, pieces, low, top_value):
    def one(position, blocks):
        draws = jax.random.uniform(jax.random.fold_in(jax.random.fold_in(stream_key, 6), position), (blocks,), jnp.float32, low / len(pieces), top_value / len(pieces))
        return jnp.repeat(jnp.exp(draws), shape[position] // blocks).reshape((-1,) + (1,) * (len(shape) - position - 1))

    loudness = one(*pieces[0])
    for cut in pieces[1:]:
        loudness = loudness * one(*cut)
    return loudness


def normal_values(own_key, dims, scale, most, shards=(), held_as=jnp.bfloat16):
    result = jax.random.normal(own_key, dims, jnp.float32) * scale
    if len(shards) > 0:
        result = block_levels(own_key, dims, shards, -0.22, 0.18) * result
    return jnp.clip(result, min=-most, max=most).astype(held_as)


def gaussian_with(own_key, extent, scale, reach, shards, heavy, held_as=jnp.bfloat16):
    result = scale * jax.random.normal(own_key, extent, jnp.float32)
    if shards:
        result = result * block_levels(own_key, extent, shards, -0.22, 0.18)
    return jnp.clip(strengthened(result, jax.random.fold_in(own_key, 3), *heavy), -reach, reach).astype(held_as)


def setup_inputs(seed: int = 0) -> dict:
    arg_keys = jax.random.split(jax.random.key(seed), 10)
    return {
        "latent": gaussian_with(arg_keys[0], (MEMBERS, LATITUDES, LONGITUDES, LATENT), 1.0, 6.0, ((0, 8), (1, 4)), (0, 3, 8, 2.0)),
        "truth": normal_values(arg_keys[1], (CHANNELS, LATITUDES, LONGITUDES), 1.0, 6.0, ((1, 4), (2, 8)), jnp.float32),
        "node_weight": jnp.clip(jnp.exp(math.log(1.0) - 1.3862944 * jax.random.uniform(arg_keys[2], (LATITUDES, LONGITUDES), jnp.float32) ** block_levels(arg_keys[2], (LATITUDES, LONGITUDES), ((0, 4), (1, 8)), -0.2, 0.2)), 0.25, 1.0),
        "first_weight": normal_values(arg_keys[3], (LATENT, HIDDEN_SIZE), LATENT ** -0.5, 0.25),
        "first_bias": normal_values(arg_keys[4], (HIDDEN_SIZE,), 0.5, 3.0, (), jnp.float32),
        "second_weight": normal_values(arg_keys[5], (HIDDEN_SIZE, HIDDEN_SIZE), HIDDEN_SIZE ** -0.5, 0.25),
        "second_bias": normal_values(arg_keys[6], (HIDDEN_SIZE,), 0.5, 3.0, (), jnp.float32),
        "out_weight": normal_values(arg_keys[7], (CHANNELS, HIDDEN_SIZE), HIDDEN_SIZE ** -0.5, 0.25),
        "out_bias": normal_values(arg_keys[8], (CHANNELS,), 0.5, 3.0, (), jnp.float32),
    }


root_half = 0.7071067811865476
density_scale = 0.3989422804014327
tap_spread = 1.5
epsilon = 1e-06
highest = lax.Precision.HIGHEST

def gelu_pair(value):
    normal_cdf = 0.5 * (1.0 + jax.scipy.special.erf(value * root_half))
    return (value * normal_cdf, normal_cdf + value * jnp.exp(-0.5 * value * value) * density_scale)

def stencil_taps(radius):
    offsets = jnp.arange(-radius, radius + 1).astype(jnp.float32)
    weights = jnp.exp(-offsets * offsets / (2.0 * tap_spread * tap_spread))
    return weights / jnp.sum(weights)

def smooth_rows(padded, taps, rows, axis):
    total = taps[0] * lax.slice_in_dim(padded, 0, rows, axis=axis)
    for offset in range(1, taps.shape[0]):
        total = total + taps[offset] * lax.slice_in_dim(padded, offset, offset + rows, axis=axis)
    return total

def score_block(ensemble, truth_block, weight_block):
    members = ensemble.shape[0]
    gram = jnp.einsum('mck,nck->kmn', ensemble, ensemble, precision=highest)
    squares = jnp.diagonal(gram, axis1=1, axis2=2)
    diagonal_mask = jnp.eye(members, dtype=bool)[None, :, :]
    distance_sq = squares[:, :, None] + squares[:, None, :] - 2.0 * gram
    distance_sq = jnp.where(diagonal_mask, 1.0, distance_sq)
    distance = jnp.sqrt(distance_sq + epsilon)
    inverse = jnp.where(diagonal_mask, 0.0, 1.0 / distance)
    spread = lax.optimization_barrier(jnp.sum(jnp.where(diagonal_mask, 0.0, distance), axis=(1, 2)))
    error = ensemble - truth_block[None, :, :]
    skill = jnp.sqrt(lax.optimization_barrier(jnp.sum(error * error, axis=1)) + epsilon)
    pair_count = members * (members - 1)
    score = lax.optimization_barrier(jnp.sum(skill, axis=0)) / members - spread / (2.0 * pair_count)
    row_total = lax.optimization_barrier(jnp.sum(inverse, axis=2))
    mixed = jnp.einsum('kmn,nck->mck', inverse, ensemble, precision=highest)
    pair_grad = ensemble * jnp.transpose(row_total)[:, None, :] - mixed
    grad = weight_block[None, None, :] * (error / (members * skill[:, None, :]) - pair_grad / pair_count)
    return (score, grad)

def forward_member(rows_in, first_weight, first_bias, second_weight, second_bias, out_weight, out_bias):
    first_pre = jnp.dot(rows_in, first_weight, preferred_element_type=jnp.float32) + first_bias
    first_act, first_slope = gelu_pair(first_pre)
    first_act = first_act.astype(jnp.bfloat16)
    second_pre = jnp.dot(first_act, second_weight, preferred_element_type=jnp.float32) + second_bias
    second_act, second_slope = gelu_pair(second_pre)
    second_act = second_act.astype(jnp.bfloat16)
    raw = jnp.dot(out_weight, second_act.T, preferred_element_type=jnp.float32) + out_bias[:, None]
    return (first_act, first_slope, second_act, second_slope, raw)

def reference(latent, truth, node_weight, first_weight, first_bias, second_weight, second_bias, out_weight, out_bias):
    taps = stencil_taps(RADIUS)
    members = latent.shape[0]
    params = (first_weight, first_bias, second_weight, second_bias, out_weight, out_bias)

    def smooth_field(field):
        padded = jnp.pad(field, ((0, 0), (RADIUS, RADIUS), (0, 0)))
        return smooth_rows(padded, taps, LATITUDES, 1)

    def member_forward(member_latent):
        rows_in = member_latent.reshape(-1, LATENT)
        raw = forward_member(rows_in, *params)[4].reshape(CHANNELS, LATITUDES, LONGITUDES)
        return smooth_field(raw).reshape(CHANNELS, CELLS)
    smoothed = lax.map(member_forward, latent)
    blocks = CELLS // SCORE_CELLS
    ens_blocks = jnp.transpose(smoothed.reshape(members, CHANNELS, blocks, SCORE_CELLS), (2, 0, 1, 3))
    truth_blocks = jnp.transpose(truth.reshape(CHANNELS, blocks, SCORE_CELLS), (1, 0, 2))
    weight_blocks = node_weight.reshape(blocks, SCORE_CELLS)

    def block_item(item):
        return score_block(item[0], item[1], item[2])
    scores, grads = lax.map(block_item, (ens_blocks, truth_blocks, weight_blocks))
    score = scores.reshape(LATITUDES, LONGITUDES)
    grad_smoothed = jnp.transpose(grads, (1, 2, 0, 3)).reshape(members, CHANNELS, CELLS)

    def member_backward(carry, item):
        member_latent, member_grad = item
        rows_in = member_latent.reshape(-1, LATENT)
        first_act, first_slope, second_act, second_slope, raw = forward_member(rows_in, *params)
        grad_raw = smooth_field(member_grad.reshape(CHANNELS, LATITUDES, LONGITUDES)).reshape(CHANNELS, CELLS)
        grad_low = grad_raw.astype(jnp.bfloat16)
        out_w_grad = jnp.dot(grad_low, second_act, preferred_element_type=jnp.float32)
        out_b_grad = lax.optimization_barrier(jnp.sum(grad_raw, axis=1))
        second_delta = jnp.dot(grad_low.T, out_weight, preferred_element_type=jnp.float32) * second_slope
        second_b_grad = lax.optimization_barrier(jnp.sum(second_delta, axis=0))
        second_low = second_delta.astype(jnp.bfloat16)
        second_w_grad = jnp.dot(first_act.T, second_low, preferred_element_type=jnp.float32)
        first_delta = jnp.dot(second_low, second_weight.T, preferred_element_type=jnp.float32) * first_slope
        first_b_grad = lax.optimization_barrier(jnp.sum(first_delta, axis=0))
        first_low = first_delta.astype(jnp.bfloat16)
        first_w_grad = jnp.dot(rows_in.T, first_low, preferred_element_type=jnp.float32)
        update = (first_w_grad, first_b_grad, second_w_grad, second_b_grad, out_w_grad, out_b_grad)
        return (tuple((old + new for old, new in zip(carry, update))), None)
    start = (jnp.zeros((LATENT, HIDDEN_SIZE), jnp.float32), jnp.zeros((HIDDEN_SIZE,), jnp.float32), jnp.zeros((HIDDEN_SIZE, HIDDEN_SIZE), jnp.float32), jnp.zeros((HIDDEN_SIZE,), jnp.float32), jnp.zeros((CHANNELS, HIDDEN_SIZE), jnp.float32), jnp.zeros((CHANNELS,), jnp.float32))
    totals, _ = lax.scan(member_backward, start, (latent, grad_smoothed))
    return (score, totals[0], totals[1], totals[2], totals[3], totals[4], totals[5])
```

```python
import functools
import math
import jax
import jax.numpy as jnp
from jax import lax
from jax.experimental import pallas as pl
from jax.experimental.pallas import tpu as pltpu
from jax.sharding import PartitionSpec as P

RADIUS = 3
LANES = 128
MESH = pl.DeviceIdType.MESH

root_half = 0.7071067811865476
density_scale = 0.3989422804014327
tap_spread = 1.5
epsilon = 1e-06


def gelu_pair(value):
    normal_cdf = 0.5 * (1.0 + lax.erf(value * root_half))
    return (value * normal_cdf, normal_cdf + value * jnp.exp(-0.5 * value * value) * density_scale)


def stencil_taps(radius):
    weights = [math.exp(-k * k / (2.0 * tap_spread * tap_spread)) for k in range(-radius, radius + 1)]
    return [w / sum(weights) for w in weights]


def remote(src, dst, send, recv, where):
    return pltpu.make_async_remote_copy(
        src_ref=src, dst_ref=dst, send_sem=send, recv_sem=recv, device_id=where, device_id_type=MESH
    )


def peer(me, p, count):
    if count & (count - 1):
        return lax.rem(me + p, count)
    total, bit = 0, 1
    while bit < count:
        total = total + lax.rem(me // bit + p // bit, 2) * bit
        bit *= 2
    return total


def smooth_block(before, own, after, taps, cols):
    edge, length = before.shape[1], own.shape[1]
    padded = jnp.concatenate([before, own, after], axis=1)
    width = padded.shape[1]
    rolled = {0: padded}
    total = None
    for index, tap in enumerate(taps):
        shift = (index - RADIUS) * cols
        rest = shift % LANES
        if rest not in rolled:
            rolled[rest] = pltpu.roll(padded, width - rest, 1)
        start = edge + shift - rest
        term = tap * rolled[rest][:, start : start + length]
        total = term if total is None else total + term
    return total


def contract(left, right, left_dim, right_dim):
    return lax.dot_general(
        left, right, (((left_dim,), (right_dim,)), ((), ())), preferred_element_type=jnp.float32
    )


def reduce_in_kernel(
    members, bands, first_sum, second_sum, small_sum, first_out, second_out, small_all,
    core_in, held, y_in, y_sum, x_wide, x_sum, x_in, y_late, pair, z_in, gather_w,
    t_core, t_held, t_y, t_ysum, t_x, t_xsum, t_z, final_s, gather_s, gather_b,
    sc, rc, sy, ry, sx, rx, sxw, rxw, syl, ryl, sz, rz, st, rt, stz, rtz, stg, rtg, sgw, rgw, sgb, rgb,
):
    me = lax.axis_index("mem")
    band = lax.axis_index("band")
    low, high = lax.rem(band, 2), band // 2
    parity, group = lax.rem(me, 2), me // 2
    groups = members // 2
    rows = first_out.shape[0]
    hidden = first_sum.shape[1]
    half, part = hidden // 2, hidden // bands
    extra = final_s.shape[0]
    partner = {"band": high * 2 + 1 - low}
    across = {"band": (1 - high) * 2 + low}
    beside = {"mem": me + 1 - 2 * parity}

    def cut(index, size):
        return pl.ds(pl.multiple_of(index * size, size), size)

    mine, other = cut(high, part), cut(1 - high, part)

    def both(q):
        return cut(q, 2 * rows)

    def kept(q):
        return cut(2 * q + parity, rows)

    def given(q):
        return cut(2 * q + 1 - parity, rows)

    def core(w, q):
        source = (second_sum, first_sum)[w]
        return remote(
            source.at[both(q), cut(1 - low, half)], core_in.at[w, both(q)], sc.at[w, q], rc.at[w, q], partner
        )

    def along_y(q):
        return remote(held.at[0, both(q), other], y_in.at[both(q)], sy.at[q], ry.at[q], across)

    def along_x(q):
        return remote(y_sum.at[given(q)], x_in.at[q], sx.at[q], rx.at[q], beside)

    def wide_x(q):
        return remote(held.at[1, given(q)], x_wide.at[q], sxw.at[q], rxw.at[q], beside)

    def late_y(q):
        return remote(x_sum.at[q, :, other], y_late.at[q], syl.at[q], ryl.at[q], across)

    def along_z(q):
        return remote(pair.at[q], z_in.at[group], sz.at[q], rz.at[group], {"mem": 2 * q + parity})

    small_core = remote(small_sum.at[:, cut(1 - low, half)], t_core, st.at[0], rt.at[0], partner)
    small_y = remote(t_held.at[:, other], t_y, st.at[1], rt.at[1], across)
    spread = groups * extra
    small_x = remote(t_ysum.at[cut(1 - parity, spread)], t_x, st.at[2], rt.at[2], beside)
    slot = parity * groups + group

    def small_z(q):
        return remote(t_xsum.at[cut(q, extra)], t_z.at[group], stz.at[q], rtz.at[group], {"mem": 2 * q + parity})

    def slot_of(k):
        return lax.rem(k, 2) * groups + k // 2

    def small_gather(k):
        return remote(final_s, gather_s.at[slot], stg.at[k], rtg.at[me], {"mem": k})

    def step_core(t, carry):
        q = peer(group, groups - 1 - t, groups)
        core(0, q).start()
        core(1, q).start()
        return carry

    small_core.start()
    lax.fori_loop(0, groups, step_core, 0)
    small_core.wait_recv()
    t_held[...] = small_sum[:, cut(low, half)] + t_core[...]
    small_y.start()

    def near(index):
        return peer(group, groups - 1 - index, groups)

    def step(t, carry):
        @pl.when(t < groups)
        def _():
            q = near(t)
            core(0, q).wait_recv()
            held[0, both(q)] = second_sum[both(q), cut(low, half)] + core_in[0, both(q)]
            along_y(q).start()
            core(1, q).wait_recv()
            held[1, both(q)] = first_sum[both(q), cut(low, half)] + core_in[1, both(q)]
            wide_x(q).start()

        @pl.when(t == 2)
        def _():
            small_y.wait_recv()
            t_ysum[...] = t_held[:, mine] + t_y[...]
            small_x.start()

        @pl.when((t >= 2) & (t < groups + 2))
        def _():
            q = near(t - 2)
            along_y(q).wait_recv()
            y_sum[both(q)] = held[0, both(q), mine] + y_in[both(q)]
            along_x(q).start()
            wide_x(q).wait_recv()
            x_sum[q] = held[1, kept(q)] + x_wide[q]
            late_y(q).start()

        @pl.when(t == 4)
        def _():
            small_x.wait_recv()
            t_xsum[...] = t_ysum[cut(parity, spread)] + t_x[...]

            def send(p, inner):
                small_z(peer(group, groups - p, groups)).start()
                return inner

            lax.fori_loop(1, groups, send, 0)

        @pl.when((t >= 4) & (t < groups + 4))
        def _():
            q = near(t - 4)
            along_x(q).wait_recv()
            pair[q, rows:] = y_sum[kept(q)] + x_in[q]
            late_y(q).wait_recv()
            pair[q, :rows] = x_sum[q, :, mine] + y_late[q]

            @pl.when(q != group)
            def _():
                along_z(q).start()

        @pl.when(t == 6)
        def _():
            def take(p, total):
                q = peer(group, p, groups)
                remote(t_z.at[q], t_z.at[q], stz.at[q], rtz.at[q], {"mem": 2 * q + parity}).wait_recv()
                return total + t_z[q]

            final_s[...] = lax.fori_loop(1, groups, take, t_xsum[cut(group, extra)])
            gather_s[slot] = final_s[...]

            def send(p, inner):
                small_gather(peer(me, members - p, members)).start()
                return inner

            lax.fori_loop(1, members, send, 0)

        return carry

    lax.fori_loop(0, max(groups, 4) + 4, step, 0)

    def weights(at, who, where):
        return remote(gather_w.at[at], gather_w.at[at], sgw.at[who], rgw.at[at], where)

    def smalls(at, who, where):
        return remote(gather_b.at[at], gather_b.at[at], sgb.at[who], rgb.at[at], where)

    far = (1 - high) * 2 + low
    near_by = high * 2 + 1 - low
    near_far = (1 - high) * 2 + 1 - low

    def take_small(p, carry):
        k = peer(me, p, members)
        at = slot_of(k)
        remote(gather_s.at[at], gather_s.at[at], stg.at[k], rtg.at[k], {"mem": k}).wait_recv()
        return carry

    lax.fori_loop(1, members, take_small, 0)
    gather_b[band] = gather_s[...]
    smalls(band, 0, across).start()
    smalls(band, 1, partner).start()

    def take_z(p, total):
        q = peer(group, groups - p, groups)
        remote(z_in.at[q], z_in.at[q], sz.at[q], rz.at[q], {"mem": 2 * q + parity}).wait_recv()
        return total + z_in[q]

    gather_w[band] = lax.fori_loop(1, groups, take_z, pair[group])
    weights(band, 0, across).start()
    weights(band, 1, partner).start()
    smalls(far, 2, across).wait_recv()
    smalls(far, 2, partner).start()
    weights(far, 2, across).wait_recv()
    weights(far, 2, partner).start()
    for at in (near_by, near_far):
        smalls(at, 0, partner).wait_recv()
        weights(at, 0, partner).wait_recv()
    for k in range(bands):
        lanes = slice((k % 2) * half + (k // 2) * part, (k % 2) * half + (k // 2) * part + part)
        first_out[:, lanes] = gather_w[k, :rows]
        second_out[:, lanes] = gather_w[k, rows:]
        small_all[:, lanes] = gather_b[k].reshape(small_all.shape[0], part)
    for at, who, where in ((band, 0, across), (band, 1, partner), (far, 2, partner)):
        weights(at, who, where).wait_send()
        smalls(at, who, where).wait_send()
    small_core.wait_send()
    small_y.wait_send()
    small_x.wait_send()

    def drain(k, carry):
        @pl.when(k != me)
        def _():
            small_gather(k).wait_send()

        return carry

    def drain_groups(q, carry):
        core(0, q).wait_send()
        core(1, q).wait_send()
        along_y(q).wait_send()
        along_x(q).wait_send()
        wide_x(q).wait_send()
        late_y(q).wait_send()

        @pl.when(q != group)
        def _():
            along_z(q).wait_send()
            small_z(q).wait_send()

        return carry

    lax.fori_loop(0, members, drain, 0)
    lax.fori_loop(0, groups, drain_groups, 0)


def reduce_scratch(members, bands, features, hidden, extra):
    groups, rows, half, part = members // 2, features // members, hidden // 2, hidden // bands
    dma = pltpu.SemaphoreType.DMA
    height = members * extra
    shapes = [
        (2, features, half), (2, features, half), (features, part), (features, part),
        (groups, rows, half), (groups, rows, half), (groups, rows, part), (groups, rows, part),
        (groups, 2 * rows, part), (groups, 2 * rows, part), (bands, 2 * rows, part),
        (height, half), (height, half), (height, part), (height, part),
        (height // 2, part), (height // 2, part), (groups, extra, part),
        (extra, part), (members, extra, part), (bands, members, extra, part),
    ]
    counts = (
        [(2, groups)] * 2 + [(groups,)] * 10 + [(3,)] * 2 + [(groups,)] * 2 + [(members,)] * 2 + [(bands,)] * 4
    )
    return [pltpu.VMEM(o, jnp.float32) for o in shapes] + [dma(n) for n in counts]


def score_kernel(
    members, bands, cols, edge,
    latent_ref, first_ref, first_bias_ref, second_ref, second_bias_ref, out_weight_ref, out_bias_ref,
    truth_in, node_ref,
    score_out, first_out, first_bias_out, second_out, second_bias_out, out_weight_out, out_bias_out,
    rows_in, first_act, first_slope, second_act, second_slope, first_sum, second_sum, small_sum, bias_sum, raw_ref,
    before, after, grad_before, grad_after, sent, ensemble, grads, back,
    halo_send, halo_recv, fwd_send, fwd_recv, ret_send, ret_recv, ghalo_send, ghalo_recv, load,
    score_ref, weight_ref, bias_column, truth_ref, small_all, *reduce_refs,
):
    me = lax.axis_index("mem")
    band = lax.axis_index("band")
    length = raw_ref.shape[2]
    rows = first_out.shape[0]
    taps = stencil_taps(RADIUS)
    has_prev = band > 0
    has_next = band < bands - 1
    prev, following = jnp.maximum(band - 1, 0), jnp.minimum(band + 1, bands - 1)

    def fetch(k):
        where = pl.ds(pl.multiple_of(k * cols, cols), cols)
        return pltpu.make_async_copy(latent_ref.at[:, where, :], rows_in.at[k], load.at[k])

    def prefetch(p, carry):
        fetch(peer(me, members - p, members)).start()
        return carry

    lax.fori_loop(1, members + 1, prefetch, 0)
    barrier = pltpu.get_barrier_semaphore()

    def greet(p, carry):
        pl.semaphore_signal(barrier, inc=1, device_id={"mem": peer(me, members - p, members)}, device_id_type=MESH)
        return carry

    lax.fori_loop(1, members, greet, 0)

    for d in range(1, bands):
        pl.semaphore_signal(barrier, inc=1, device_id={"band": lax.rem(band + d, bands)}, device_id_type=MESH)
    channels, hidden = out_weight_ref.shape
    shape = (channels, channels)
    diagonal = lax.broadcasted_iota(jnp.int32, shape, 0) == lax.broadcasted_iota(jnp.int32, shape, 1)
    bias_column[...] = jnp.sum(jnp.where(diagonal, out_bias_ref[...], 0.0), axis=1, keepdims=True)
    truth_ref[...] = truth_in[...].reshape(length, channels).T
    for row in range(node_ref.shape[0]):
        weight_ref[:, row * cols : (row + 1) * cols] = node_ref[row : row + 1, :]
    pl.semaphore_wait(barrier, members + bands - 2)

    @pl.when(band == 0)
    def _():
        before[...] = jnp.zeros_like(before)
        grad_before[...] = jnp.zeros_like(grad_before)

    @pl.when(band == bands - 1)
    def _():
        after[...] = jnp.zeros_like(after)
        grad_after[...] = jnp.zeros_like(grad_after)

    def to_next(source, target, k, send, recv):
        return remote(source.at[k, :, pl.ds(length - edge, edge)], target.at[k], send.at[0, k], recv.at[0, k], {"band": following})

    def to_prev(source, target, k, send, recv):
        return remote(source.at[k, :, pl.ds(0, edge)], target.at[k], send.at[1, k], recv.at[1, k], {"band": prev})

    def start_edges(source, low, high, k, send, recv):
        @pl.when(has_next)
        def _():
            to_next(source, low, k, send, recv).start()

        @pl.when(has_prev)
        def _():
            to_prev(source, high, k, send, recv).start()

    def wait_edges(source, low, high, k, send, recv):
        @pl.when(has_prev)
        def _():
            to_next(source, low, k, send, recv).wait_recv()

        @pl.when(has_next)
        def _():
            to_prev(source, high, k, send, recv).wait_recv()

    def drain_edges(source, low, high, k, send, recv):
        @pl.when(has_next)
        def _():
            to_next(source, low, k, send, recv).wait_send()

        @pl.when(has_prev)
        def _():
            to_prev(source, high, k, send, recv).wait_send()

    raw_edges = (raw_ref, before, after)
    grad_edges = (back, grad_before, grad_after)

    def forward(k):
        return remote(sent.at[k], ensemble.at[me], fwd_send.at[k], fwd_recv.at[me], {"mem": k})

    def returning(k):
        return remote(grads.at[k], back.at[me], ret_send.at[k], ret_recv.at[me], {"mem": k})

    def arrived(buffer, sems, k):
        remote(buffer.at[k], buffer.at[k], sems.at[k], sems.at[k], {"mem": k}).wait_recv()

    def decode(k):
        fetch(k).wait()
        inputs = rows_in[k].reshape(length, rows_in.shape[3])
        pre = jnp.dot(inputs, first_ref[...], preferred_element_type=jnp.float32) + first_bias_ref[...]
        act, slope = gelu_pair(pre)
        first_act[k] = act.astype(jnp.bfloat16)
        first_slope[k] = slope
        pre = jnp.dot(first_act[k], second_ref[...], preferred_element_type=jnp.float32) + second_bias_ref[...]
        act, slope = gelu_pair(pre)
        second_act[k] = act.astype(jnp.bfloat16)
        second_slope[k] = slope
        raw_ref[k] = contract(out_weight_ref[...], second_act[k], 1, 1) + bias_column[...]

    def spread(p):
        k = peer(me, members - p, members)
        wait_edges(*raw_edges, k, halo_send, halo_recv)
        smooth = smooth_block(before[k], raw_ref[k], after[k], taps, cols)

        @pl.when(p < members)
        def _():
            sent[k] = smooth
            forward(k).start()

        @pl.when(p == members)
        def _():
            ensemble[k] = smooth

    def forward_step(p, carry):
        @pl.when(p <= members)
        def _():
            k = peer(me, members - p, members)
            decode(k)
            start_edges(*raw_edges, k, halo_send, halo_recv)

        @pl.when(p >= 2)
        def _():
            spread(p - 1)

        return carry

    lax.fori_loop(1, members + 2, forward_step, 0)

    def collect(p, carry):
        arrived(ensemble, fwd_recv, peer(me, p, members))
        return carry

    lax.fori_loop(1, members, collect, 0)
    score_ref[...] = jnp.zeros_like(score_ref)
    pair_count = members * (members - 1)
    row_ids = lax.broadcasted_iota(jnp.int32, (members, LANES), 0)

    def member(p, carry):
        m = peer(me, members - p, members)

        def chunk(c, inner):
            lanes = pl.ds(pl.multiple_of(c * LANES, LANES), LANES)
            mine = ensemble[m, :, lanes]
            gaps = mine[None] - ensemble[:, :, lanes]
            distance = jnp.sqrt(jnp.sum(gaps * gaps, axis=1) + epsilon)
            own = row_ids == m
            inverse = jnp.where(own, 0.0, 1.0 / distance)
            spread_sum = jnp.sum(jnp.where(own, 0.0, distance), axis=0, keepdims=True)
            pair_grad = jnp.sum(gaps * inverse[:, None, :], axis=0)
            error = mine - truth_ref[:, lanes]
            skill = jnp.sqrt(jnp.sum(error * error, axis=0, keepdims=True) + epsilon)
            score_ref[:, lanes] += skill / members - spread_sum / (2.0 * pair_count)
            result = weight_ref[:, lanes] * (error / (members * skill) - pair_grad / pair_count)

            @pl.when(p < members)
            def _():
                grads[m, :, lanes] = result

            @pl.when(p == members)
            def _():
                back[m, :, lanes] = result

            return inner

        lax.fori_loop(0, length // LANES, chunk, 0)

        @pl.when(p < members)
        def _():
            returning(m).start()

        return carry

    lax.fori_loop(1, members + 1, member, 0)
    start_edges(*grad_edges, me, ghalo_send, ghalo_recv)

    first_sum[...] = jnp.zeros_like(first_sum)
    second_sum[...] = jnp.zeros_like(second_sum)
    small_sum[...] = jnp.zeros_like(small_sum)
    bias_sum[...] = jnp.zeros_like(bias_sum)

    def finish(p):
        k = peer(me, p, members)
        wait_edges(*grad_edges, k, ghalo_send, ghalo_recv)
        grad_raw = smooth_block(grad_before[k], back[k], grad_after[k], taps, cols)
        grad_low = grad_raw.astype(jnp.bfloat16)
        bias_sum[...] += jnp.sum(grad_raw, axis=1, keepdims=True)
        small_sum[:channels] += jnp.dot(grad_low, second_act[k], preferred_element_type=jnp.float32)
        delta = contract(grad_low, out_weight_ref[...], 0, 0) * second_slope[k]
        small_sum[channels + 1 : channels + 2] += jnp.sum(delta, axis=0, keepdims=True)
        low = delta.astype(jnp.bfloat16)
        second_sum[...] += contract(first_act[k], low, 0, 0)
        delta = contract(low, second_ref[...], 1, 1) * first_slope[k]
        small_sum[channels : channels + 1] += jnp.sum(delta, axis=0, keepdims=True)
        inputs = rows_in[k].reshape(length, rows_in.shape[3])
        first_sum[...] += contract(inputs, delta.astype(jnp.bfloat16), 0, 0)

    def backward_step(p, carry):
        @pl.when(p < members)
        def _():
            k = peer(me, p, members)
            arrived(back, ret_recv, k)
            start_edges(*grad_edges, k, ghalo_send, ghalo_recv)

        finish(p - 1)
        return carry

    lax.fori_loop(1, members + 1, backward_step, 0)
    small_sum[channels + 2 : channels + 3, :channels] = jnp.sum(
        jnp.where(diagonal, bias_sum[...], 0.0), axis=0, keepdims=True
    )
    reduce_in_kernel(
        members, bands, first_sum, second_sum, small_sum, first_out, second_out, small_all, *reduce_refs
    )
    for row in range(score_out.shape[0]):
        score_out[row : row + 1, :] = score_ref[:, row * cols : (row + 1) * cols]
    out_weight_out[...] = small_all[:channels]
    first_bias_out[...] = small_all[channels : channels + 1]
    second_bias_out[...] = small_all[channels + 1 : channels + 2]
    out_bias_out[...] = small_all[channels + 2 : channels + 3, :channels]

    def drain(k, carry):
        drain_edges(*raw_edges, k, halo_send, halo_recv)
        drain_edges(*grad_edges, k, ghalo_send, ghalo_recv)

        @pl.when(k != me)
        def _():
            forward(k).wait_send()
            returning(k).wait_send()

        return carry

    lax.fori_loop(0, members, drain, 0)


def score_and_gradient(latent, weights, truth, weight, members, bands, cols, rows, extra):
    lat_rows, _, features = latent.shape
    channels, length = truth.shape[2], lat_rows * cols
    hidden = weights[0].shape[1]
    edge = min(length, -(-RADIUS * cols // LANES) * LANES)
    block = (members, channels, length)
    halo = (members, channels, edge)
    units = (members, length, hidden)
    dma = pltpu.SemaphoreType.DMA
    vmem = pl.BlockSpec(memory_space=pltpu.VMEM)
    single, half = jnp.float32, jnp.bfloat16
    return pl.pallas_call(
        functools.partial(score_kernel, members, bands, cols, edge),
        out_shape=tuple(
            jax.ShapeDtypeStruct(o, single)
            for o in (
                (lat_rows, cols), (rows, hidden), (1, hidden), (rows, hidden), (1, hidden),
                (channels, hidden), (1, channels),
            )
        ),
        in_specs=[pl.BlockSpec(memory_space=pl.ANY)] + [vmem] * 8,
        out_specs=(vmem,) * 7,
        scratch_shapes=[
            pltpu.VMEM((members, lat_rows, cols, features), half),
            pltpu.VMEM(units, half), pltpu.VMEM(units, single),
            pltpu.VMEM(units, half), pltpu.VMEM(units, single),
            pltpu.VMEM((features, hidden), single), pltpu.VMEM((hidden, hidden), single),
            pltpu.VMEM((members * extra, hidden), single), pltpu.VMEM((channels, 1), single),
            pltpu.VMEM(block, single),
        ]
        + [pltpu.VMEM(halo, single)] * 4
        + [pltpu.VMEM(block, single)] * 4
        + [dma((2, members))] * 2
        + [dma((members,))] * 4
        + [dma((2, members))] * 2
        + [dma((members,))]
        + [pltpu.VMEM(o, single) for o in [
            (1, length), (1, length), (channels, 1), (channels, length), (members * extra, hidden),
        ]]
        + reduce_scratch(members, bands, features, hidden, extra),
        compiler_params=pltpu.CompilerParams(collective_id=0, has_side_effects=True, vmem_limit_bytes=60 << 20),
    )(latent, *weights, truth, weight)


def write_kernel(*refs):
    count = len(refs) // 2
    for source, target in zip(refs[:count], refs[count:]):
        target[...] = source[...]


def write_results(values):
    vmem = pl.BlockSpec(memory_space=pltpu.VMEM)
    return pl.pallas_call(
        write_kernel,
        out_shape=tuple(jax.ShapeDtypeStruct(v.shape, v.dtype) for v in values),
        in_specs=[vmem] * len(values),
        out_specs=(vmem,) * len(values),
    )(*values)


def body(
    latent, truth, node_weight, first_weight, first_bias, second_weight, second_bias, out_weight, out_bias
):
    members, bands = lax.axis_size("mem"), lax.axis_size("band")
    _, lat_rows, lon_cols, features = latent.shape
    channels, hidden = out_weight.shape
    cols = lon_cols // members
    rows = features // members
    extra = -(-(channels + 3) // (8 * members)) * 8
    weights = (
        first_weight, first_bias[None], second_weight, second_bias[None], out_weight, out_bias[None]
    )
    score, first, first_b, second, second_b, out_w, out_b = write_results(score_and_gradient(
        latent.reshape(lat_rows, lon_cols, features), weights,
        jnp.transpose(truth, (1, 2, 0)), node_weight, members, bands, cols, rows, extra,
    ))
    return (score, first, first_b[0], second, second_b[0], out_w, out_b[0])


def solution(mesh):
    in_specs = (
        P("mem", "band", None, None),
        P(None, "band", "mem"),
        P("band", "mem"),
        P(),
        P(),
        P(),
        P(),
        P(),
        P(),
    )
    out_specs = (P("band", "mem"), P("mem", None), P(), P("mem", None), P(), P(), P())
    return jax.shard_map(body, mesh=mesh, in_specs=in_specs, out_specs=out_specs, check_vma=False)
```

```python
import functools
import math
import jax
import jax.numpy as jnp
from jax import lax
from jax.experimental import pallas as pl
from jax.experimental.pallas import tpu as pltpu
from jax.sharding import PartitionSpec as P

RADIUS = 3
LANES = 128
MESH = pl.DeviceIdType.MESH

root_half = 0.7071067811865476
density_scale = 0.3989422804014327
tap_spread = 1.5
epsilon = 1e-06


def gelu_pair(value):
    normal_cdf = 0.5 * (1.0 + lax.erf(value * root_half))
    return (value * normal_cdf, normal_cdf + value * jnp.exp(-0.5 * value * value) * density_scale)


def stencil_taps(radius):
    weights = [math.exp(-k * k / (2.0 * tap_spread * tap_spread)) for k in range(-radius, radius + 1)]
    return [w / sum(weights) for w in weights]


def remote(src, dst, send, recv, where):
    return pltpu.make_async_remote_copy(
        src_ref=src, dst_ref=dst, send_sem=send, recv_sem=recv, device_id=where, device_id_type=MESH
    )


def peer(me, p, count):
    if count & (count - 1):
        return lax.rem(me + p, count)
    total, bit = 0, 1
    while bit < count:
        total = total + lax.rem(me // bit + p // bit, 2) * bit
        bit *= 2
    return total


def smooth_block(before, own, after, taps, cols):
    edge, length = before.shape[1], own.shape[1]
    padded = jnp.concatenate([before, own, after], axis=1)
    width = padded.shape[1]
    rolled = {0: padded}
    total = None
    for index, tap in enumerate(taps):
        shift = (index - RADIUS) * cols
        rest = shift % LANES
        if rest not in rolled:
            rolled[rest] = pltpu.roll(padded, width - rest, 1)
        start = edge + shift - rest
        term = tap * rolled[rest][:, start : start + length]
        total = term if total is None else total + term
    return total


def contract(left, right, left_dim, right_dim):
    return lax.dot_general(
        left, right, (((left_dim,), (right_dim,)), ((), ())), preferred_element_type=jnp.float32
    )


def reduce_in_kernel(
    members, bands, first_sum, second_sum, small_sum, first_out, second_out, small_all,
    core_in, held, y_in, y_sum, x_wide, x_sum, x_in, y_late, pair, z_in, gather_w,
    t_core, t_held, t_y, t_ysum, t_x, t_xsum, t_z, final_s, gather_s, gather_b,
    sc, rc, sy, ry, sx, rx, sxw, rxw, syl, ryl, sz, rz, st, rt, stz, rtz, stg, rtg, sgw, rgw, sgb, rgb,
):
    me = lax.axis_index("mem")
    band = lax.axis_index("band")
    low, high = lax.rem(band, 2), band // 2
    parity, group = lax.rem(me, 2), me // 2
    groups = members // 2
    rows = first_out.shape[0]
    hidden = first_sum.shape[1]
    half, part = hidden // 2, hidden // bands
    extra = final_s.shape[0]
    partner = {"band": high * 2 + 1 - low}
    across = {"band": (1 - high) * 2 + low}
    beside = {"mem": me + 1 - 2 * parity}

    def cut(index, size):
        return pl.ds(pl.multiple_of(index * size, size), size)

    mine, other = cut(high, part), cut(1 - high, part)

    def both(q):
        return cut(q, 2 * rows)

    def kept(q):
        return cut(2 * q + parity, rows)

    def given(q):
        return cut(2 * q + 1 - parity, rows)

    def core(w, q):
        source = (second_sum, first_sum)[w]
        return remote(
            source.at[both(q), cut(1 - low, half)], core_in.at[w, both(q)], sc.at[w, q], rc.at[w, q], partner
        )

    def along_y(q):
        return remote(held.at[0, both(q), other], y_in.at[both(q)], sy.at[q], ry.at[q], across)

    def along_x(q):
        return remote(y_sum.at[given(q)], x_in.at[q], sx.at[q], rx.at[q], beside)

    def wide_x(q):
        return remote(held.at[1, given(q)], x_wide.at[q], sxw.at[q], rxw.at[q], beside)

    def late_y(q):
        return remote(x_sum.at[q, :, other], y_late.at[q], syl.at[q], ryl.at[q], across)

    def along_z(q):
        return remote(pair.at[q], z_in.at[group], sz.at[q], rz.at[group], {"mem": 2 * q + parity})

    small_core = remote(small_sum.at[:, cut(1 - low, half)], t_core, st.at[0], rt.at[0], partner)
    small_y = remote(t_held.at[:, other], t_y, st.at[1], rt.at[1], across)
    spread = groups * extra
    small_x = remote(t_ysum.at[cut(1 - parity, spread)], t_x, st.at[2], rt.at[2], beside)
    slot = parity * groups + group

    def small_z(q):
        return remote(t_xsum.at[cut(q, extra)], t_z.at[group], stz.at[q], rtz.at[group], {"mem": 2 * q + parity})

    def slot_of(k):
        return lax.rem(k, 2) * groups + k // 2

    def small_gather(k):
        return remote(final_s, gather_s.at[slot], stg.at[k], rtg.at[me], {"mem": k})

    def step_core(t, carry):
        q = peer(group, groups - 1 - t, groups)
        core(0, q).start()
        core(1, q).start()
        return carry

    small_core.start()
    lax.fori_loop(0, groups, step_core, 0)
    small_core.wait_recv()
    t_held[...] = small_sum[:, cut(low, half)] + t_core[...]
    small_y.start()

    def near(index):
        return peer(group, groups - 1 - index, groups)

    def step(t, carry):
        @pl.when(t < groups)
        def _():
            q = near(t)
            core(0, q).wait_recv()
            held[0, both(q)] = second_sum[both(q), cut(low, half)] + core_in[0, both(q)]
            along_y(q).start()
            core(1, q).wait_recv()
            held[1, both(q)] = first_sum[both(q), cut(low, half)] + core_in[1, both(q)]
            wide_x(q).start()

        @pl.when(t == 2)
        def _():
            small_y.wait_recv()
            t_ysum[...] = t_held[:, mine] + t_y[...]
            small_x.start()

        @pl.when((t >= 2) & (t < groups + 2))
        def _():
            q = near(t - 2)
            along_y(q).wait_recv()
            y_sum[both(q)] = held[0, both(q), mine] + y_in[both(q)]
            along_x(q).start()
            wide_x(q).wait_recv()
            x_sum[q] = held[1, kept(q)] + x_wide[q]
            late_y(q).start()

        @pl.when(t == 4)
        def _():
            small_x.wait_recv()
            t_xsum[...] = t_ysum[cut(parity, spread)] + t_x[...]

            def send(p, inner):
                small_z(peer(group, groups - p, groups)).start()
                return inner

            lax.fori_loop(1, groups, send, 0)

        @pl.when((t >= 4) & (t < groups + 4))
        def _():
            q = near(t - 4)
            along_x(q).wait_recv()
            pair[q, rows:] = y_sum[kept(q)] + x_in[q]
            late_y(q).wait_recv()
            pair[q, :rows] = x_sum[q, :, mine] + y_late[q]

            @pl.when(q != group)
            def _():
                along_z(q).start()

        @pl.when(t == 6)
        def _():
            def take(p, total):
                q = peer(group, p, groups)
                remote(t_z.at[q], t_z.at[q], stz.at[q], rtz.at[q], {"mem": 2 * q + parity}).wait_recv()
                return total + t_z[q]

            final_s[...] = lax.fori_loop(1, groups, take, t_xsum[cut(group, extra)])
            gather_s[slot] = final_s[...]

            def send(p, inner):
                small_gather(peer(me, members - p, members)).start()
                return inner

            lax.fori_loop(1, members, send, 0)

        return carry

    lax.fori_loop(0, max(groups, 4) + 4, step, 0)

    def weights(at, who, where):
        return remote(gather_w.at[at], gather_w.at[at], sgw.at[who], rgw.at[at], where)

    def smalls(at, who, where):
        return remote(gather_b.at[at], gather_b.at[at], sgb.at[who], rgb.at[at], where)

    far = (1 - high) * 2 + low
    near_by = high * 2 + 1 - low
    near_far = (1 - high) * 2 + 1 - low

    def take_small(p, carry):
        k = peer(me, p, members)
        at = slot_of(k)
        remote(gather_s.at[at], gather_s.at[at], stg.at[k], rtg.at[k], {"mem": k}).wait_recv()
        return carry

    lax.fori_loop(1, members, take_small, 0)
    gather_b[band] = gather_s[...]
    smalls(band, 0, across).start()
    smalls(band, 1, partner).start()

    def take_z(p, total):
        q = peer(group, groups - p, groups)
        remote(z_in.at[q], z_in.at[q], sz.at[q], rz.at[q], {"mem": 2 * q + parity}).wait_recv()
        return total + z_in[q]

    gather_w[band] = lax.fori_loop(1, groups, take_z, pair[group])
    weights(band, 0, across).start()
    weights(band, 1, partner).start()
    smalls(far, 2, across).wait_recv()
    smalls(far, 2, partner).start()
    weights(far, 2, across).wait_recv()
    weights(far, 2, partner).start()
    for at in (near_by, near_far):
        smalls(at, 0, partner).wait_recv()
        weights(at, 0, partner).wait_recv()
    for k in range(bands):
        lanes = slice((k % 2) * half + (k // 2) * part, (k % 2) * half + (k // 2) * part + part)
        first_out[:, lanes] = gather_w[k, :rows]
        second_out[:, lanes] = gather_w[k, rows:]
        small_all[:, lanes] = gather_b[k].reshape(small_all.shape[0], part)
    for at, who, where in ((band, 0, across), (band, 1, partner), (far, 2, partner)):
        weights(at, who, where).wait_send()
        smalls(at, who, where).wait_send()
    small_core.wait_send()
    small_y.wait_send()
    small_x.wait_send()

    def drain(k, carry):
        @pl.when(k != me)
        def _():
            small_gather(k).wait_send()

        return carry

    def drain_groups(q, carry):
        core(0, q).wait_send()
        core(1, q).wait_send()
        along_y(q).wait_send()
        along_x(q).wait_send()
        wide_x(q).wait_send()
        late_y(q).wait_send()

        @pl.when(q != group)
        def _():
            along_z(q).wait_send()
            small_z(q).wait_send()

        return carry

    lax.fori_loop(0, members, drain, 0)
    lax.fori_loop(0, groups, drain_groups, 0)


def reduce_scratch(members, bands, features, hidden, extra):
    groups, rows, half, part = members // 2, features // members, hidden // 2, hidden // bands
    dma = pltpu.SemaphoreType.DMA
    height = members * extra
    shapes = [
        (2, features, half), (2, features, half), (features, part), (features, part),
        (groups, rows, half), (groups, rows, half), (groups, rows, part), (groups, rows, part),
        (groups, 2 * rows, part), (groups, 2 * rows, part), (bands, 2 * rows, part),
        (height, half), (height, half), (height, part), (height, part),
        (height // 2, part), (height // 2, part), (groups, extra, part),
        (extra, part), (members, extra, part), (bands, members, extra, part),
    ]
    counts = (
        [(2, groups)] * 2 + [(groups,)] * 10 + [(3,)] * 2 + [(groups,)] * 2 + [(members,)] * 2 + [(bands,)] * 4
    )
    return [pltpu.VMEM(o, jnp.float32) for o in shapes] + [dma(n) for n in counts]


def score_kernel(
    members, bands, chunks, cols, edge,
    latent_ref, first_ref, first_bias_ref, second_ref, second_bias_ref, out_weight_ref, out_bias_ref,
    truth_in, node_ref,
    score_out, first_out, first_bias_out, second_out, second_bias_out, out_weight_out, out_bias_out,
    rows_in, first_act, first_slope, second_act, second_slope, first_sum, second_sum, small_sum, bias_sum, raw_ref,
    before, after, grad_before, grad_after, sent, ensemble, grads, returned, back,
    halo_send, halo_recv, ghalo_send, ghalo_recv, fwd_send, fwd_recv, ret_send, ret_recv, load,
    score_ref, weight_ref, truth_ref, bias_column, small_all, *reduce_refs,
):
    me = lax.axis_index("mem")
    band = lax.axis_index("band")
    length = raw_ref.shape[2]
    lat_rows = node_ref.shape[0]
    blocks = chunks * members
    taps = stencil_taps(RADIUS)
    has_prev = band > 0
    has_next = band < bands - 1
    prev, following = jnp.maximum(band - 1, 0), jnp.minimum(band + 1, bands - 1)

    def outward(s):
        return peer(me, members - 1 - lax.rem(s, members), members)

    def inward(s):
        return peer(me, lax.rem(s, members), members)

    def block_of(s, k):
        return (s // members) * members + k

    def fetch(s):
        chunk, k = s // members, outward(s)
        where = pl.ds(pl.multiple_of((k * chunks + chunk) * cols, cols), cols)
        b = block_of(s, k)
        return pltpu.make_async_copy(latent_ref.at[:, where, :], rows_in.at[b], load.at[b])

    def prefetch(s, carry):
        fetch(s).start()
        return carry

    lax.fori_loop(0, blocks, prefetch, 0)
    barrier = pltpu.get_barrier_semaphore()

    def greet(p, carry):
        pl.semaphore_signal(barrier, inc=1, device_id={"mem": peer(me, members - p, members)}, device_id_type=MESH)
        return carry

    lax.fori_loop(1, members, greet, 0)

    for d in range(1, bands):
        pl.semaphore_signal(barrier, inc=1, device_id={"band": lax.rem(band + d, bands)}, device_id_type=MESH)
    channels, hidden = out_weight_ref.shape
    shape = (channels, channels)
    diagonal = lax.broadcasted_iota(jnp.int32, shape, 0) == lax.broadcasted_iota(jnp.int32, shape, 1)
    bias_column[...] = jnp.sum(jnp.where(diagonal, out_bias_ref[...], 0.0), axis=1, keepdims=True)
    for c in range(chunks):
        truth_ref[c] = truth_in[:, c * cols : (c + 1) * cols, :].reshape(length, channels).T
        for row in range(lat_rows):
            weight_ref[c, :, row * cols : (row + 1) * cols] = node_ref[row : row + 1, c * cols : (c + 1) * cols]

    @pl.when(band == 0)
    def _():
        before[...] = jnp.zeros_like(before)
        grad_before[...] = jnp.zeros_like(grad_before)

    @pl.when(band == bands - 1)
    def _():
        after[...] = jnp.zeros_like(after)
        grad_after[...] = jnp.zeros_like(grad_after)

    pl.semaphore_wait(barrier, members + bands - 2)

    def to_next(source, target, b, send, recv):
        return remote(source.at[b, :, pl.ds(length - edge, edge)], target.at[b], send.at[0, b], recv.at[0, b], {"band": following})

    def to_prev(source, target, b, send, recv):
        return remote(source.at[b, :, pl.ds(0, edge)], target.at[b], send.at[1, b], recv.at[1, b], {"band": prev})

    def start_edges(source, low, high, b, send, recv):
        @pl.when(has_next)
        def _():
            to_next(source, low, b, send, recv).start()

        @pl.when(has_prev)
        def _():
            to_prev(source, high, b, send, recv).start()

    def wait_edges(source, low, high, b, send, recv):
        @pl.when(has_prev)
        def _():
            to_next(source, low, b, send, recv).wait_recv()

        @pl.when(has_next)
        def _():
            to_prev(source, high, b, send, recv).wait_recv()

    def drain_edges(source, low, high, b, send, recv):
        @pl.when(has_next)
        def _():
            to_next(source, low, b, send, recv).wait_send()

        @pl.when(has_prev)
        def _():
            to_prev(source, high, b, send, recv).wait_send()

    raw_edges = (raw_ref, before, after)
    grad_edges = (grads, grad_before, grad_after)

    def forward(s, k):
        b = block_of(s, k)
        return remote(sent.at[b], ensemble.at[block_of(s, me)], fwd_send.at[b], fwd_recv.at[block_of(s, me)], {"mem": k})

    def returning(s, k):
        b = block_of(s, k)
        return remote(returned.at[b], back.at[block_of(s, me)], ret_send.at[b], ret_recv.at[block_of(s, me)], {"mem": k})

    def arrived(buffer, sems, s, k):
        b = block_of(s, k)
        remote(buffer.at[b], buffer.at[b], sems.at[b], sems.at[b], {"mem": k}).wait_recv()

    def decode(s):
        b = block_of(s, outward(s))
        fetch(s).wait()
        inputs = rows_in[b].reshape(length, rows_in.shape[3])
        pre = jnp.dot(inputs, first_ref[...], preferred_element_type=jnp.float32) + first_bias_ref[...]
        act, slope = gelu_pair(pre)
        first_act[b] = act.astype(jnp.bfloat16)
        first_slope[b] = slope
        pre = jnp.dot(first_act[b], second_ref[...], preferred_element_type=jnp.float32) + second_bias_ref[...]
        act, slope = gelu_pair(pre)
        second_act[b] = act.astype(jnp.bfloat16)
        second_slope[b] = slope
        raw_ref[b] = contract(out_weight_ref[...], second_act[b], 1, 1) + bias_column[...]
        start_edges(*raw_edges, b, halo_send, halo_recv)

    def spread(s):
        k = outward(s)
        b = block_of(s, k)
        wait_edges(*raw_edges, b, halo_send, halo_recv)
        smooth = smooth_block(before[b], raw_ref[b], after[b], taps, cols)

        @pl.when(k != me)
        def _():
            sent[b] = smooth
            forward(s, k).start()

        @pl.when(k == me)
        def _():
            ensemble[b] = smooth

    lag = 2

    def forward_step(s, carry):
        @pl.when(s < blocks)
        def _():
            decode(s)

        @pl.when(s >= lag)
        def _():
            spread(s - lag)

        return carry

    lax.fori_loop(0, blocks + lag, forward_step, 0)
    first_sum[...] = jnp.zeros_like(first_sum)
    second_sum[...] = jnp.zeros_like(second_sum)
    small_sum[...] = jnp.zeros_like(small_sum)
    bias_sum[...] = jnp.zeros_like(bias_sum)
    score_ref[...] = jnp.zeros_like(score_ref)
    pair_count = members * (members - 1)
    row_ids = lax.broadcasted_iota(jnp.int32, (members, LANES), 0)

    def score_chunk(c, carry):
        start = c * members

        def collect(p, inner):
            arrived(ensemble, fwd_recv, start, peer(me, p, members))
            return inner

        lax.fori_loop(1, members, collect, 0)

        def member(p, inner):
            m = outward(p)
            b = start + m

            def piece(i, innermost):
                lanes = pl.ds(pl.multiple_of(i * LANES, LANES), LANES)
                mine = ensemble[b, :, lanes]
                gaps = mine[None] - ensemble[pl.ds(start, members), :, lanes]
                distance = jnp.sqrt(jnp.sum(gaps * gaps, axis=1) + epsilon)
                own = row_ids == m
                inverse = jnp.where(own, 0.0, 1.0 / distance)
                spread_sum = jnp.sum(jnp.where(own, 0.0, distance), axis=0, keepdims=True)
                pair_grad = jnp.sum(gaps * inverse[:, None, :], axis=0)
                error = mine - truth_ref[c, :, lanes]
                skill = jnp.sqrt(jnp.sum(error * error, axis=0, keepdims=True) + epsilon)
                score_ref[c, :, lanes] += skill / members - spread_sum / (2.0 * pair_count)
                grads[b, :, lanes] = weight_ref[c, :, lanes] * (error / (members * skill) - pair_grad / pair_count)
                return innermost

            lax.fori_loop(0, length // LANES, piece, 0)
            start_edges(*grad_edges, b, ghalo_send, ghalo_recv)
            return inner

        lax.fori_loop(0, members, member, 0)

        def give(p, inner):
            m = outward(p)
            b = start + m
            wait_edges(*grad_edges, b, ghalo_send, ghalo_recv)
            smooth = smooth_block(grad_before[b], grads[b], grad_after[b], taps, cols)

            @pl.when(m != me)
            def _():
                returned[b] = smooth
                returning(start, m).start()

            @pl.when(m == me)
            def _():
                back[b] = smooth

            return inner

        lax.fori_loop(0, members, give, 0)
        return carry

    lax.fori_loop(0, chunks, score_chunk, 0)

    def finish(s, carry):
        k = inward(s)
        b = block_of(s, k)

        @pl.when(k != me)
        def _():
            arrived(back, ret_recv, s, k)

        grad_raw = back[b]
        grad_low = grad_raw.astype(jnp.bfloat16)
        bias_sum[...] += jnp.sum(grad_raw, axis=1, keepdims=True)
        small_sum[:channels] += jnp.dot(grad_low, second_act[b], preferred_element_type=jnp.float32)
        delta = contract(grad_low, out_weight_ref[...], 0, 0) * second_slope[b]
        small_sum[channels + 1 : channels + 2] += jnp.sum(delta, axis=0, keepdims=True)
        low = delta.astype(jnp.bfloat16)
        second_sum[...] += contract(first_act[b], low, 0, 0)
        delta = contract(low, second_ref[...], 1, 1) * first_slope[b]
        small_sum[channels : channels + 1] += jnp.sum(delta, axis=0, keepdims=True)
        inputs = rows_in[b].reshape(length, rows_in.shape[3])
        first_sum[...] += contract(inputs, delta.astype(jnp.bfloat16), 0, 0)
        return carry

    lax.fori_loop(0, blocks, finish, 0)
    small_sum[channels + 2 : channels + 3, :channels] = jnp.sum(
        jnp.where(diagonal, bias_sum[...], 0.0), axis=0, keepdims=True
    )
    reduce_in_kernel(
        members, bands, first_sum, second_sum, small_sum, first_out, second_out, small_all, *reduce_refs
    )
    for c in range(chunks):
        for row in range(lat_rows):
            score_out[row : row + 1, c * cols : (c + 1) * cols] = score_ref[c, :, row * cols : (row + 1) * cols]
    out_weight_out[...] = small_all[:channels]
    first_bias_out[...] = small_all[channels : channels + 1]
    second_bias_out[...] = small_all[channels + 1 : channels + 2]
    out_bias_out[...] = small_all[channels + 2 : channels + 3, :channels]

    def drain(s, carry):
        k = inward(s)
        b = block_of(s, k)
        drain_edges(*raw_edges, b, halo_send, halo_recv)
        drain_edges(*grad_edges, b, ghalo_send, ghalo_recv)

        @pl.when(k != me)
        def _():
            forward(s, k).wait_send()
            returning(s, k).wait_send()

        return carry

    lax.fori_loop(0, blocks, drain, 0)


def score_and_gradient(latent, weights, truth, weight, members, bands, cols, rows, extra):
    lat_rows, _, features = latent.shape
    channels = truth.shape[2]
    hidden = weights[0].shape[1]
    chunks = 2 if cols % 32 == 0 and lat_rows * cols % (2 * LANES) == 0 else 1
    part_cols = cols // chunks
    length = lat_rows * part_cols
    edge = min(length, -(-RADIUS * part_cols // LANES) * LANES)
    blocks = chunks * members
    block = (blocks, channels, length)
    halo = (blocks, channels, edge)
    units = (blocks, length, hidden)
    dma = pltpu.SemaphoreType.DMA
    vmem = pl.BlockSpec(memory_space=pltpu.VMEM)
    single, half = jnp.float32, jnp.bfloat16
    return pl.pallas_call(
        functools.partial(score_kernel, members, bands, chunks, part_cols, edge),
        out_shape=tuple(
            jax.ShapeDtypeStruct(o, single)
            for o in (
                (lat_rows, cols), (rows, hidden), (1, hidden), (rows, hidden), (1, hidden),
                (channels, hidden), (1, channels),
            )
        ),
        in_specs=[pl.BlockSpec(memory_space=pl.ANY)] + [vmem] * 8,
        out_specs=(vmem,) * 7,
        scratch_shapes=[
            pltpu.VMEM((blocks, lat_rows, part_cols, features), half),
            pltpu.VMEM(units, half), pltpu.VMEM(units, single),
            pltpu.VMEM(units, half), pltpu.VMEM(units, single),
            pltpu.VMEM((features, hidden), single), pltpu.VMEM((hidden, hidden), single),
            pltpu.VMEM((members * extra, hidden), single), pltpu.VMEM((channels, 1), single),
            pltpu.VMEM(block, single),
        ]
        + [pltpu.VMEM(halo, single)] * 4
        + [pltpu.VMEM(block, single)] * 5
        + [dma((2, blocks))] * 4
        + [dma((blocks,))] * 5
        + [pltpu.VMEM(o, single) for o in [
            (chunks, 1, length), (chunks, 1, length), (chunks, channels, length), (channels, 1),
            (members * extra, hidden),
        ]]
        + reduce_scratch(members, bands, features, hidden, extra),
        compiler_params=pltpu.CompilerParams(collective_id=0, has_side_effects=True, vmem_limit_bytes=60 << 20),
    )(latent, *weights, truth, weight)


def write_kernel(*refs):
    count = len(refs) // 2
    for source, target in zip(refs[:count], refs[count:]):
        target[...] = source[...]


def write_results(values):
    vmem = pl.BlockSpec(memory_space=pltpu.VMEM)
    return pl.pallas_call(
        write_kernel,
        out_shape=tuple(jax.ShapeDtypeStruct(v.shape, v.dtype) for v in values),
        in_specs=[vmem] * len(values),
        out_specs=(vmem,) * len(values),
    )(*values)


def body(
    latent, truth, node_weight, first_weight, first_bias, second_weight, second_bias, out_weight, out_bias
):
    members, bands = lax.axis_size("mem"), lax.axis_size("band")
    _, lat_rows, lon_cols, features = latent.shape
    channels, hidden = out_weight.shape
    cols = lon_cols // members
    rows = features // members
    extra = -(-(channels + 3) // (8 * members)) * 8
    weights = (
        first_weight, first_bias[None], second_weight, second_bias[None], out_weight, out_bias[None]
    )
    score, first, first_b, second, second_b, out_w, out_b = write_results(score_and_gradient(
        latent.reshape(lat_rows, lon_cols, features), weights,
        jnp.transpose(truth, (1, 2, 0)), node_weight, members, bands, cols, rows, extra,
    ))
    return (score, first, first_b[0], second, second_b[0], out_w, out_b[0])


def solution(mesh):
    in_specs = (
        P("mem", "band", None, None),
        P(None, "band", "mem"),
        P("band", "mem"),
        P(),
        P(),
        P(),
        P(),
        P(),
        P(),
    )
    out_specs = (P("band", "mem"), P("mem", None), P(), P("mem", None), P(), P(), P())
    return jax.shard_map(body, mesh=mesh, in_specs=in_specs, out_specs=out_specs, check_vma=False)
```

```python
import functools
import math
import jax
import jax.numpy as jnp
from jax import lax
from jax.experimental import pallas as pl
from jax.experimental.pallas import tpu as pltpu
from jax.sharding import PartitionSpec as P

RADIUS = 3
LANES = 128
MESH = pl.DeviceIdType.MESH

root_half = 0.7071067811865476
density_scale = 0.3989422804014327
tap_spread = 1.5
epsilon = 1e-06


def gelu_pair(value):
    normal_cdf = 0.5 * (1.0 + lax.erf(value * root_half))
    return (value * normal_cdf, normal_cdf + value * jnp.exp(-0.5 * value * value) * density_scale)


def stencil_taps(radius):
    weights = [math.exp(-k * k / (2.0 * tap_spread * tap_spread)) for k in range(-radius, radius + 1)]
    return [w / sum(weights) for w in weights]


def remote(src, dst, send, recv, where):
    return pltpu.make_async_remote_copy(
        src_ref=src, dst_ref=dst, send_sem=send, recv_sem=recv, device_id=where, device_id_type=MESH
    )


def peer(me, p, count):
    if count & (count - 1):
        return lax.rem(me + p, count)
    total, bit = 0, 1
    while bit < count:
        total = total + lax.rem(me // bit + p // bit, 2) * bit
        bit *= 2
    return total


def smooth_block(before, own, after, taps, cols):
    edge, length = before.shape[1], own.shape[1]
    padded = jnp.concatenate([before, own, after], axis=1)
    width = padded.shape[1]
    rolled = {0: padded}
    total = None
    for index, tap in enumerate(taps):
        shift = (index - RADIUS) * cols
        rest = shift % LANES
        if rest not in rolled:
            rolled[rest] = pltpu.roll(padded, width - rest, 1)
        start = edge + shift - rest
        term = tap * rolled[rest][:, start : start + length]
        total = term if total is None else total + term
    return total


def contract(left, right, left_dim, right_dim):
    return lax.dot_general(
        left, right, (((left_dim,), (right_dim,)), ((), ())), preferred_element_type=jnp.float32
    )


def reduce_in_kernel(
    members, bands, first_sum, second_sum, small_sum, first_out, second_out, small_all,
    core_in, held, y_in, y_sum, x_wide, x_sum, x_in, y_late, pair, z_in, gather_w,
    t_core, t_held, t_y, t_ysum, t_x, t_xsum, t_z, final_s, gather_s, gather_b,
    sc, rc, sy, ry, sx, rx, sxw, rxw, syl, ryl, sz, rz, st, rt, stz, rtz, stg, rtg, sgw, rgw, sgb, rgb,
):
    me = lax.axis_index("mem")
    band = lax.axis_index("band")
    low, high = lax.rem(band, 2), band // 2
    parity, group = lax.rem(me, 2), me // 2
    groups = members // 2
    rows = first_out.shape[0]
    hidden = first_sum.shape[1]
    half, part = hidden // 2, hidden // bands
    extra = final_s.shape[0]
    partner = {"band": high * 2 + 1 - low}
    across = {"band": (1 - high) * 2 + low}
    beside = {"mem": me + 1 - 2 * parity}

    def cut(index, size):
        return pl.ds(pl.multiple_of(index * size, size), size)

    mine, other = cut(high, part), cut(1 - high, part)

    def both(q):
        return cut(q, 2 * rows)

    def kept(q):
        return cut(2 * q + parity, rows)

    def given(q):
        return cut(2 * q + 1 - parity, rows)

    def core(w, q):
        source = (second_sum, first_sum)[w]
        return remote(
            source.at[both(q), cut(1 - low, half)], core_in.at[w, both(q)], sc.at[w, q], rc.at[w, q], partner
        )

    def along_y(q):
        return remote(held.at[0, both(q), other], y_in.at[both(q)], sy.at[q], ry.at[q], across)

    def along_x(q):
        return remote(y_sum.at[given(q)], x_in.at[q], sx.at[q], rx.at[q], beside)

    def wide_x(q):
        return remote(held.at[1, given(q)], x_wide.at[q], sxw.at[q], rxw.at[q], beside)

    def late_y(q):
        return remote(x_sum.at[q, :, other], y_late.at[q], syl.at[q], ryl.at[q], across)

    def along_z(q):
        return remote(pair.at[q], z_in.at[group], sz.at[q], rz.at[group], {"mem": 2 * q + parity})

    small_core = remote(small_sum.at[:, cut(1 - low, half)], t_core, st.at[0], rt.at[0], partner)
    small_y = remote(t_held.at[:, other], t_y, st.at[1], rt.at[1], across)
    spread = groups * extra
    small_x = remote(t_ysum.at[cut(1 - parity, spread)], t_x, st.at[2], rt.at[2], beside)
    slot = parity * groups + group

    def small_z(q):
        return remote(t_xsum.at[cut(q, extra)], t_z.at[group], stz.at[q], rtz.at[group], {"mem": 2 * q + parity})

    def slot_of(k):
        return lax.rem(k, 2) * groups + k // 2

    def small_gather(k):
        return remote(final_s, gather_s.at[slot], stg.at[k], rtg.at[me], {"mem": k})

    def step_core(t, carry):
        q = peer(group, groups - 1 - t, groups)
        core(0, q).start()
        core(1, q).start()
        return carry

    small_core.start()
    lax.fori_loop(0, groups, step_core, 0)
    small_core.wait_recv()
    t_held[...] = small_sum[:, cut(low, half)] + t_core[...]
    small_y.start()

    def near(index):
        return peer(group, groups - 1 - index, groups)

    def step(t, carry):
        @pl.when(t < groups)
        def _():
            q = near(t)
            core(0, q).wait_recv()
            held[0, both(q)] = second_sum[both(q), cut(low, half)] + core_in[0, both(q)]
            along_y(q).start()
            core(1, q).wait_recv()
            held[1, both(q)] = first_sum[both(q), cut(low, half)] + core_in[1, both(q)]
            wide_x(q).start()

        @pl.when(t == 2)
        def _():
            small_y.wait_recv()
            t_ysum[...] = t_held[:, mine] + t_y[...]
            small_x.start()

        @pl.when((t >= 2) & (t < groups + 2))
        def _():
            q = near(t - 2)
            along_y(q).wait_recv()
            y_sum[both(q)] = held[0, both(q), mine] + y_in[both(q)]
            along_x(q).start()
            wide_x(q).wait_recv()
            x_sum[q] = held[1, kept(q)] + x_wide[q]
            late_y(q).start()

        @pl.when(t == 4)
        def _():
            small_x.wait_recv()
            t_xsum[...] = t_ysum[cut(parity, spread)] + t_x[...]

            def send(p, inner):
                small_z(peer(group, groups - p, groups)).start()
                return inner

            lax.fori_loop(1, groups, send, 0)

        @pl.when((t >= 4) & (t < groups + 4))
        def _():
            q = near(t - 4)
            along_x(q).wait_recv()
            pair[q, rows:] = y_sum[kept(q)] + x_in[q]
            late_y(q).wait_recv()
            pair[q, :rows] = x_sum[q, :, mine] + y_late[q]

            @pl.when(q != group)
            def _():
                along_z(q).start()

        @pl.when(t == 6)
        def _():
            def take(p, total):
                q = peer(group, p, groups)
                remote(t_z.at[q], t_z.at[q], stz.at[q], rtz.at[q], {"mem": 2 * q + parity}).wait_recv()
                return total + t_z[q]

            final_s[...] = lax.fori_loop(1, groups, take, t_xsum[cut(group, extra)])
            gather_s[slot] = final_s[...]

            def send(p, inner):
                small_gather(peer(me, members - p, members)).start()
                return inner

            lax.fori_loop(1, members, send, 0)

        return carry

    lax.fori_loop(0, max(groups, 4) + 4, step, 0)

    def weights(at, who, where):
        return remote(gather_w.at[at], gather_w.at[at], sgw.at[who], rgw.at[at], where)

    def smalls(at, who, where):
        return remote(gather_b.at[at], gather_b.at[at], sgb.at[who], rgb.at[at], where)

    far = (1 - high) * 2 + low
    near_by = high * 2 + 1 - low
    near_far = (1 - high) * 2 + 1 - low

    def take_small(p, carry):
        k = peer(me, p, members)
        at = slot_of(k)
        remote(gather_s.at[at], gather_s.at[at], stg.at[k], rtg.at[k], {"mem": k}).wait_recv()
        return carry

    lax.fori_loop(1, members, take_small, 0)
    gather_b[band] = gather_s[...]
    smalls(band, 0, across).start()
    smalls(band, 1, partner).start()

    def take_z(p, total):
        q = peer(group, groups - p, groups)
        remote(z_in.at[q], z_in.at[q], sz.at[q], rz.at[q], {"mem": 2 * q + parity}).wait_recv()
        return total + z_in[q]

    gather_w[band] = lax.fori_loop(1, groups, take_z, pair[group])
    weights(band, 0, across).start()
    weights(band, 1, partner).start()
    smalls(far, 2, across).wait_recv()
    smalls(far, 2, partner).start()
    weights(far, 2, across).wait_recv()
    weights(far, 2, partner).start()
    for at in (near_by, near_far):
        smalls(at, 0, partner).wait_recv()
        weights(at, 0, partner).wait_recv()
    for k in range(bands):
        lanes = slice((k % 2) * half + (k // 2) * part, (k % 2) * half + (k // 2) * part + part)
        first_out[:, lanes] = gather_w[k, :rows]
        second_out[:, lanes] = gather_w[k, rows:]
        small_all[:, lanes] = gather_b[k].reshape(small_all.shape[0], part)
    for at, who, where in ((band, 0, across), (band, 1, partner), (far, 2, partner)):
        weights(at, who, where).wait_send()
        smalls(at, who, where).wait_send()
    small_core.wait_send()
    small_y.wait_send()
    small_x.wait_send()

    def drain(k, carry):
        @pl.when(k != me)
        def _():
            small_gather(k).wait_send()

        return carry

    def drain_groups(q, carry):
        core(0, q).wait_send()
        core(1, q).wait_send()
        along_y(q).wait_send()
        along_x(q).wait_send()
        wide_x(q).wait_send()
        late_y(q).wait_send()

        @pl.when(q != group)
        def _():
            along_z(q).wait_send()
            small_z(q).wait_send()

        return carry

    lax.fori_loop(0, members, drain, 0)
    lax.fori_loop(0, groups, drain_groups, 0)


def reduce_scratch(members, bands, features, hidden, extra):
    groups, rows, half, part = members // 2, features // members, hidden // 2, hidden // bands
    dma = pltpu.SemaphoreType.DMA
    height = members * extra
    shapes = [
        (2, features, half), (2, features, half), (features, part), (features, part),
        (groups, rows, half), (groups, rows, half), (groups, rows, part), (groups, rows, part),
        (groups, 2 * rows, part), (groups, 2 * rows, part), (bands, 2 * rows, part),
        (height, half), (height, half), (height, part), (height, part),
        (height // 2, part), (height // 2, part), (groups, extra, part),
        (extra, part), (members, extra, part), (bands, members, extra, part),
    ]
    counts = (
        [(2, groups)] * 2 + [(groups,)] * 10 + [(3,)] * 2 + [(groups,)] * 2 + [(members,)] * 2 + [(bands,)] * 4
    )
    return [pltpu.VMEM(o, jnp.float32) for o in shapes] + [dma(n) for n in counts]


def score_kernel(
    members, bands, chunks, cols, edge,
    latent_ref, first_hbm, first_bias_hbm, second_hbm, second_bias_hbm, out_weight_hbm, out_bias_hbm,
    truth_hbm, node_hbm,
    score_out, first_out, first_bias_out, second_out, second_bias_out, out_weight_out, out_bias_out,
    first_ref, first_bias_ref, second_ref, second_bias_ref, out_weight_ref, out_bias_ref, truth_in, node_ref, inputs_sem,
    rows_in, first_act, first_slope, second_act, second_slope, first_sum, second_sum, small_sum, bias_sum, raw_ref,
    before, after, grad_before, grad_after, sent, ensemble, grads, returned, back,
    halo_send, halo_recv, ghalo_send, ghalo_recv, fwd_send, fwd_recv, ret_send, ret_recv, load,
    score_ref, weight_ref, truth_ref, bias_column, small_all, *reduce_refs,
):
    me = lax.axis_index("mem")
    band = lax.axis_index("band")
    length = raw_ref.shape[2]
    lat_rows = node_ref.shape[0]
    blocks = chunks * members
    taps = stencil_taps(RADIUS)
    has_prev = band > 0
    has_next = band < bands - 1
    prev, following = jnp.maximum(band - 1, 0), jnp.minimum(band + 1, bands - 1)

    def outward(s):
        return peer(me, members - 1 - lax.rem(s, members), members)

    def inward(s):
        return peer(me, lax.rem(s, members), members)

    def block_of(s, k):
        return (s // members) * members + k

    def fetch(s):
        chunk, k = s // members, outward(s)
        where = pl.ds(pl.multiple_of((k * chunks + chunk) * cols, cols), cols)
        b = block_of(s, k)
        return pltpu.make_async_copy(latent_ref.at[:, where, :], rows_in.at[b], load.at[b])

    def prefetch(s, carry):
        fetch(s).start()
        return carry

    barrier = pltpu.get_barrier_semaphore()

    def greet(p, carry):
        pl.semaphore_signal(barrier, inc=1, device_id={"mem": peer(me, members - p, members)}, device_id_type=MESH)
        return carry

    lax.fori_loop(1, members, greet, 0)

    for d in range(1, bands):
        pl.semaphore_signal(barrier, inc=1, device_id={"band": lax.rem(band + d, bands)}, device_id_type=MESH)

    pairs = (
        (first_hbm, first_ref), (first_bias_hbm, first_bias_ref), (second_hbm, second_ref),
        (second_bias_hbm, second_bias_ref), (out_weight_hbm, out_weight_ref), (out_bias_hbm, out_bias_ref),
        (truth_hbm, truth_in), (node_hbm, node_ref),
    )
    loads = [pltpu.make_async_copy(source, target, inputs_sem.at[i]) for i, (source, target) in enumerate(pairs)]
    for copy in loads[:2]:
        copy.start()
    fetch(0).start()
    for copy in loads[2:6]:
        copy.start()
    lax.fori_loop(1, blocks, prefetch, 0)
    for copy in loads[6:]:
        copy.start()
    channels, hidden = out_weight_ref.shape
    @pl.when(band == 0)
    def _():
        before[...] = jnp.zeros_like(before)
        grad_before[...] = jnp.zeros_like(grad_before)

    @pl.when(band == bands - 1)
    def _():
        after[...] = jnp.zeros_like(after)
        grad_after[...] = jnp.zeros_like(grad_after)

    def to_next(source, target, b, send, recv):
        return remote(source.at[b, :, pl.ds(length - edge, edge)], target.at[b], send.at[0, b], recv.at[0, b], {"band": following})

    def to_prev(source, target, b, send, recv):
        return remote(source.at[b, :, pl.ds(0, edge)], target.at[b], send.at[1, b], recv.at[1, b], {"band": prev})

    def start_edges(source, low, high, b, send, recv):
        @pl.when(has_next)
        def _():
            to_next(source, low, b, send, recv).start()

        @pl.when(has_prev)
        def _():
            to_prev(source, high, b, send, recv).start()

    def wait_edges(source, low, high, b, send, recv):
        @pl.when(has_prev)
        def _():
            to_next(source, low, b, send, recv).wait_recv()

        @pl.when(has_next)
        def _():
            to_prev(source, high, b, send, recv).wait_recv()

    def drain_edges(source, low, high, b, send, recv):
        @pl.when(has_next)
        def _():
            to_next(source, low, b, send, recv).wait_send()

        @pl.when(has_prev)
        def _():
            to_prev(source, high, b, send, recv).wait_send()

    raw_edges = (raw_ref, before, after)
    grad_edges = (grads, grad_before, grad_after)

    def forward(s, k):
        b = block_of(s, k)
        return remote(sent.at[b], ensemble.at[block_of(s, me)], fwd_send.at[b], fwd_recv.at[block_of(s, me)], {"mem": k})

    def returning(s, k):
        b = block_of(s, k)
        return remote(returned.at[b], back.at[block_of(s, me)], ret_send.at[b], ret_recv.at[block_of(s, me)], {"mem": k})

    def arrived(buffer, sems, s, k):
        b = block_of(s, k)
        remote(buffer.at[b], buffer.at[b], sems.at[b], sems.at[b], {"mem": k}).wait_recv()

    def decode(s):
        b = block_of(s, outward(s))
        fetch(s).wait()
        inputs = rows_in[b].reshape(length, rows_in.shape[3])
        pre = jnp.dot(inputs, first_ref[...], preferred_element_type=jnp.float32) + first_bias_ref[...]
        act, slope = gelu_pair(pre)
        first_act[b] = act.astype(jnp.bfloat16)
        first_slope[b] = slope
        pre = jnp.dot(first_act[b], second_ref[...], preferred_element_type=jnp.float32) + second_bias_ref[...]
        act, slope = gelu_pair(pre)
        second_act[b] = act.astype(jnp.bfloat16)
        second_slope[b] = slope
        raw_ref[b] = contract(out_weight_ref[...], second_act[b], 1, 1) + bias_column[...]

    def decode_edges(s):
        start_edges(*raw_edges, block_of(s, outward(s)), halo_send, halo_recv)

    def spread(s):
        k = outward(s)
        b = block_of(s, k)
        wait_edges(*raw_edges, b, halo_send, halo_recv)
        smooth = smooth_block(before[b], raw_ref[b], after[b], taps, cols)

        @pl.when(k != me)
        def _():
            sent[b] = smooth
            forward(s, k).start()

        @pl.when(k == me)
        def _():
            ensemble[b] = smooth

    lead = 2

    def early_step(s, carry):
        decode(s)
        return carry

    def early_edges(s, carry):
        decode_edges(s)
        return carry

    def forward_step(s, carry):
        @pl.when(s < blocks)
        def _():
            decode(s)
            decode_edges(s)

        spread(s - lead)
        return carry

    for copy in loads[:6]:
        copy.wait()
    shape = (channels, channels)
    diagonal = lax.broadcasted_iota(jnp.int32, shape, 0) == lax.broadcasted_iota(jnp.int32, shape, 1)
    bias_column[...] = jnp.sum(jnp.where(diagonal, out_bias_ref[...], 0.0), axis=1, keepdims=True)
    lax.fori_loop(0, lead, early_step, 0)
    pl.semaphore_wait(barrier, members + bands - 2)
    lax.fori_loop(0, lead, early_edges, 0)
    lax.fori_loop(lead, blocks + lead, forward_step, 0)
    for copy in loads[6:]:
        copy.wait()
    for c in range(chunks):
        truth_ref[c] = truth_in[:, c * cols : (c + 1) * cols, :].reshape(length, channels).T
        for row in range(lat_rows):
            weight_ref[c, :, row * cols : (row + 1) * cols] = node_ref[row : row + 1, c * cols : (c + 1) * cols]
    first_sum[...] = jnp.zeros_like(first_sum)
    second_sum[...] = jnp.zeros_like(second_sum)
    small_sum[...] = jnp.zeros_like(small_sum)
    bias_sum[...] = jnp.zeros_like(bias_sum)
    score_ref[...] = jnp.zeros_like(score_ref)
    pair_count = members * (members - 1)
    row_ids = lax.broadcasted_iota(jnp.int32, (members, LANES), 0)

    def score_chunk(c, carry):
        start = c * members

        def collect(p, inner):
            arrived(ensemble, fwd_recv, start, peer(me, p, members))
            return inner

        lax.fori_loop(1, members, collect, 0)

        def member(p, inner):
            m = outward(p)
            b = start + m

            def piece(i, innermost):
                lanes = pl.ds(pl.multiple_of(i * LANES, LANES), LANES)
                mine = ensemble[b, :, lanes]
                gaps = mine[None] - ensemble[pl.ds(start, members), :, lanes]
                distance = jnp.sqrt(jnp.sum(gaps * gaps, axis=1) + epsilon)
                own = row_ids == m
                inverse = jnp.where(own, 0.0, 1.0 / distance)
                spread_sum = jnp.sum(jnp.where(own, 0.0, distance), axis=0, keepdims=True)
                pair_grad = jnp.sum(gaps * inverse[:, None, :], axis=0)
                error = mine - truth_ref[c, :, lanes]
                skill = jnp.sqrt(jnp.sum(error * error, axis=0, keepdims=True) + epsilon)
                score_ref[c, :, lanes] += skill / members - spread_sum / (2.0 * pair_count)
                grads[b, :, lanes] = weight_ref[c, :, lanes] * (error / (members * skill) - pair_grad / pair_count)
                return innermost

            lax.fori_loop(0, length // LANES, piece, 0)
            start_edges(*grad_edges, b, ghalo_send, ghalo_recv)
            return inner

        lax.fori_loop(0, members, member, 0)

        def give(p, inner):
            m = outward(p)
            b = start + m
            wait_edges(*grad_edges, b, ghalo_send, ghalo_recv)
            smooth = smooth_block(grad_before[b], grads[b], grad_after[b], taps, cols)

            @pl.when(m != me)
            def _():
                returned[b] = smooth
                returning(start, m).start()

            @pl.when(m == me)
            def _():
                back[b] = smooth

            return inner

        lax.fori_loop(0, members, give, 0)
        return carry

    lax.fori_loop(0, chunks, score_chunk, 0)

    def finish(s, carry):
        k = inward(s)
        b = block_of(s, k)

        @pl.when(k != me)
        def _():
            arrived(back, ret_recv, s, k)

        grad_raw = back[b]
        grad_low = grad_raw.astype(jnp.bfloat16)
        bias_sum[...] += jnp.sum(grad_raw, axis=1, keepdims=True)
        small_sum[:channels] += jnp.dot(grad_low, second_act[b], preferred_element_type=jnp.float32)
        delta = contract(grad_low, out_weight_ref[...], 0, 0) * second_slope[b]
        small_sum[channels + 1 : channels + 2] += jnp.sum(delta, axis=0, keepdims=True)
        low = delta.astype(jnp.bfloat16)
        second_sum[...] += contract(first_act[b], low, 0, 0)
        delta = contract(low, second_ref[...], 1, 1) * first_slope[b]
        small_sum[channels : channels + 1] += jnp.sum(delta, axis=0, keepdims=True)
        inputs = rows_in[b].reshape(length, rows_in.shape[3])
        first_sum[...] += contract(inputs, delta.astype(jnp.bfloat16), 0, 0)
        return carry

    lax.fori_loop(0, blocks, finish, 0)
    small_sum[channels + 2 : channels + 3, :channels] = jnp.sum(
        jnp.where(diagonal, bias_sum[...], 0.0), axis=0, keepdims=True
    )
    reduce_in_kernel(
        members, bands, first_sum, second_sum, small_sum, first_out, second_out, small_all, *reduce_refs
    )
    for c in range(chunks):
        for row in range(lat_rows):
            score_out[row : row + 1, c * cols : (c + 1) * cols] = score_ref[c, :, row * cols : (row + 1) * cols]
    out_weight_out[...] = small_all[:channels]
    first_bias_out[...] = small_all[channels : channels + 1]
    second_bias_out[...] = small_all[channels + 1 : channels + 2]
    out_bias_out[...] = small_all[channels + 2 : channels + 3, :channels]

    def drain(s, carry):
        k = inward(s)
        b = block_of(s, k)
        drain_edges(*raw_edges, b, halo_send, halo_recv)
        drain_edges(*grad_edges, b, ghalo_send, ghalo_recv)

        @pl.when(k != me)
        def _():
            forward(s, k).wait_send()
            returning(s, k).wait_send()

        return carry

    lax.fori_loop(0, blocks, drain, 0)


def score_and_gradient(latent, weights, truth, weight, members, bands, cols, rows, extra):
    lat_rows, _, features = latent.shape
    channels = truth.shape[2]
    hidden = weights[0].shape[1]
    chunks = 2 if cols % 32 == 0 and lat_rows * cols % (2 * LANES) == 0 else 1
    part_cols = cols // chunks
    length = lat_rows * part_cols
    edge = min(length, -(-RADIUS * part_cols // LANES) * LANES)
    blocks = chunks * members
    block = (blocks, channels, length)
    halo = (blocks, channels, edge)
    units = (blocks, length, hidden)
    dma = pltpu.SemaphoreType.DMA
    vmem = pl.BlockSpec(memory_space=pltpu.VMEM)
    single, half = jnp.float32, jnp.bfloat16
    return pl.pallas_call(
        functools.partial(score_kernel, members, bands, chunks, part_cols, edge),
        out_shape=tuple(
            jax.ShapeDtypeStruct(o, single)
            for o in (
                (lat_rows, cols), (rows, hidden), (1, hidden), (rows, hidden), (1, hidden),
                (channels, hidden), (1, channels),
            )
        ),
        in_specs=[pl.BlockSpec(memory_space=pl.ANY)] * 9,
        out_specs=(vmem,) * 7,
        scratch_shapes=[pltpu.VMEM(v.shape, v.dtype) for v in (*weights, truth, weight)]
        + [dma((8,))]
        + [
            pltpu.VMEM((blocks, lat_rows, part_cols, features), half),
            pltpu.VMEM(units, half), pltpu.VMEM(units, single),
            pltpu.VMEM(units, half), pltpu.VMEM(units, single),
            pltpu.VMEM((features, hidden), single), pltpu.VMEM((hidden, hidden), single),
            pltpu.VMEM((members * extra, hidden), single), pltpu.VMEM((channels, 1), single),
            pltpu.VMEM(block, single),
        ]
        + [pltpu.VMEM(halo, single)] * 4
        + [pltpu.VMEM(block, single)] * 5
        + [dma((2, blocks))] * 4
        + [dma((blocks,))] * 5
        + [pltpu.VMEM(o, single) for o in [
            (chunks, 1, length), (chunks, 1, length), (chunks, channels, length), (channels, 1),
            (members * extra, hidden),
        ]]
        + reduce_scratch(members, bands, features, hidden, extra),
        compiler_params=pltpu.CompilerParams(collective_id=0, has_side_effects=True, vmem_limit_bytes=60 << 20),
    )(latent, *weights, truth, weight)


def write_kernel(*refs):
    count = len(refs) // 2
    for source, target in zip(refs[:count], refs[count:]):
        target[...] = source[...]


def write_results(values):
    vmem = pl.BlockSpec(memory_space=pltpu.VMEM)
    return pl.pallas_call(
        write_kernel,
        out_shape=tuple(jax.ShapeDtypeStruct(v.shape, v.dtype) for v in values),
        in_specs=[vmem] * len(values),
        out_specs=(vmem,) * len(values),
    )(*values)


def body(
    latent, truth, node_weight, first_weight, first_bias, second_weight, second_bias, out_weight, out_bias
):
    members, bands = lax.axis_size("mem"), lax.axis_size("band")
    _, lat_rows, lon_cols, features = latent.shape
    channels, hidden = out_weight.shape
    cols = lon_cols // members
    rows = features // members
    extra = -(-(channels + 3) // (8 * members)) * 8
    weights = (
        first_weight, first_bias[None], second_weight, second_bias[None], out_weight, out_bias[None]
    )
    score, first, first_b, second, second_b, out_w, out_b = write_results(score_and_gradient(
        latent.reshape(lat_rows, lon_cols, features), weights,
        jnp.transpose(truth, (1, 2, 0)), node_weight, members, bands, cols, rows, extra,
    ))
    return (score, first, first_b[0], second, second_b[0], out_w, out_b[0])


def solution(mesh):
    in_specs = (
        P("mem", "band", None, None),
        P(None, "band", "mem"),
        P("band", "mem"),
        P(),
        P(),
        P(),
        P(),
        P(),
        P(),
    )
    out_specs = (P("band", "mem"), P("mem", None), P(), P("mem", None), P(), P(), P())
    return jax.shard_map(body, mesh=mesh, in_specs=in_specs, out_specs=out_specs, check_vma=False)
```

```python
import functools
import math
import jax
import jax.numpy as jnp
from jax import lax
from jax.experimental import pallas as pl
from jax.experimental.pallas import tpu as pltpu
from jax.sharding import PartitionSpec as P

RADIUS = 3
LANES = 128
MESH = pl.DeviceIdType.MESH

root_half = 0.7071067811865476
density_scale = 0.3989422804014327
tap_spread = 1.5
epsilon = 1e-06


def gelu_pair(value):
    normal_cdf = 0.5 * (1.0 + lax.erf(value * root_half))
    return (value * normal_cdf, normal_cdf + value * jnp.exp(-0.5 * value * value) * density_scale)


def stencil_taps(radius):
    weights = [math.exp(-k * k / (2.0 * tap_spread * tap_spread)) for k in range(-radius, radius + 1)]
    return [w / sum(weights) for w in weights]


def remote(src, dst, send, recv, where):
    return pltpu.make_async_remote_copy(
        src_ref=src, dst_ref=dst, send_sem=send, recv_sem=recv, device_id=where, device_id_type=MESH
    )


def peer(me, p, count):
    if count & (count - 1):
        return lax.rem(me + p, count)
    total, bit = 0, 1
    while bit < count:
        total = total + lax.rem(me // bit + p // bit, 2) * bit
        bit *= 2
    return total


def smooth_block(before, own, after, taps, cols):
    edge, length = before.shape[1], own.shape[1]
    padded = jnp.concatenate([before, own, after], axis=1)
    width = padded.shape[1]
    rolled = {0: padded}
    total = None
    for index, tap in enumerate(taps):
        shift = (index - RADIUS) * cols
        rest = shift % LANES
        if rest not in rolled:
            rolled[rest] = pltpu.roll(padded, width - rest, 1)
        start = edge + shift - rest
        term = tap * rolled[rest][:, start : start + length]
        total = term if total is None else total + term
    return total


def contract(left, right, left_dim, right_dim):
    return lax.dot_general(
        left, right, (((left_dim,), (right_dim,)), ((), ())), preferred_element_type=jnp.float32
    )


def reduce_in_kernel(
    members, bands, first_sum, second_sum, small_sum, first_out, second_out, small_all,
    core_in, held, y_in, y_sum, x_wide, x_sum, x_in, y_late, pair, z_in, gather_w,
    t_core, t_held, t_y, t_ysum, t_x, t_xsum, t_z, final_s, gather_s, gather_b,
    sc, rc, sy, ry, sx, rx, sxw, rxw, syl, ryl, sz, rz, st, rt, stz, rtz, stg, rtg, sgw, rgw, sgb, rgb,
):
    me = lax.axis_index("mem")
    band = lax.axis_index("band")
    low, high = lax.rem(band, 2), band // 2
    parity, group = lax.rem(me, 2), me // 2
    groups = members // 2
    rows = first_out.shape[0]
    hidden = first_sum.shape[1]
    half, part = hidden // 2, hidden // bands
    extra = final_s.shape[0]
    partner = {"band": high * 2 + 1 - low}
    across = {"band": (1 - high) * 2 + low}
    beside = {"mem": me + 1 - 2 * parity}

    def cut(index, size):
        return pl.ds(pl.multiple_of(index * size, size), size)

    mine, other = cut(high, part), cut(1 - high, part)

    def both(q):
        return cut(q, 2 * rows)

    def kept(q):
        return cut(2 * q + parity, rows)

    def given(q):
        return cut(2 * q + 1 - parity, rows)

    def core(w, q):
        source = (second_sum, first_sum)[w]
        return remote(
            source.at[both(q), cut(1 - low, half)], core_in.at[w, both(q)], sc.at[w, q], rc.at[w, q], partner
        )

    def along_y(q):
        return remote(held.at[0, both(q), other], y_in.at[both(q)], sy.at[q], ry.at[q], across)

    def along_x(q):
        return remote(y_sum.at[given(q)], x_in.at[q], sx.at[q], rx.at[q], beside)

    def wide_x(q):
        return remote(held.at[1, given(q)], x_wide.at[q], sxw.at[q], rxw.at[q], beside)

    def late_y(q):
        return remote(x_sum.at[q, :, other], y_late.at[q], syl.at[q], ryl.at[q], across)

    def along_z(q):
        return remote(pair.at[q], z_in.at[group], sz.at[q], rz.at[group], {"mem": 2 * q + parity})

    small_core = remote(small_sum.at[:, cut(1 - low, half)], t_core, st.at[0], rt.at[0], partner)
    small_y = remote(t_held.at[:, other], t_y, st.at[1], rt.at[1], across)
    spread = groups * extra
    small_x = remote(t_ysum.at[cut(1 - parity, spread)], t_x, st.at[2], rt.at[2], beside)
    slot = parity * groups + group

    def small_z(q):
        return remote(t_xsum.at[cut(q, extra)], t_z.at[group], stz.at[q], rtz.at[group], {"mem": 2 * q + parity})

    def slot_of(k):
        return lax.rem(k, 2) * groups + k // 2

    def small_gather(k):
        return remote(final_s, gather_s.at[slot], stg.at[k], rtg.at[me], {"mem": k})

    def step_core(t, carry):
        q = peer(group, groups - 1 - t, groups)
        core(0, q).start()
        core(1, q).start()
        return carry

    small_core.start()
    lax.fori_loop(0, groups, step_core, 0)
    small_core.wait_recv()
    t_held[...] = small_sum[:, cut(low, half)] + t_core[...]
    small_y.start()

    def near(index):
        return peer(group, groups - 1 - index, groups)

    def step(t, carry):
        @pl.when(t < groups)
        def _():
            q = near(t)
            core(0, q).wait_recv()
            held[0, both(q)] = second_sum[both(q), cut(low, half)] + core_in[0, both(q)]
            along_y(q).start()
            core(1, q).wait_recv()
            held[1, both(q)] = first_sum[both(q), cut(low, half)] + core_in[1, both(q)]
            wide_x(q).start()

        @pl.when(t == 2)
        def _():
            small_y.wait_recv()
            t_ysum[...] = t_held[:, mine] + t_y[...]
            small_x.start()

        @pl.when((t >= 2) & (t < groups + 2))
        def _():
            q = near(t - 2)
            along_y(q).wait_recv()
            y_sum[both(q)] = held[0, both(q), mine] + y_in[both(q)]
            along_x(q).start()
            wide_x(q).wait_recv()
            x_sum[q] = held[1, kept(q)] + x_wide[q]
            late_y(q).start()

        @pl.when(t == 4)
        def _():
            small_x.wait_recv()
            t_xsum[...] = t_ysum[cut(parity, spread)] + t_x[...]

            def send(p, inner):
                small_z(peer(group, groups - p, groups)).start()
                return inner

            lax.fori_loop(1, groups, send, 0)

        @pl.when((t >= 4) & (t < groups + 4))
        def _():
            q = near(t - 4)
            along_x(q).wait_recv()
            pair[q, rows:] = y_sum[kept(q)] + x_in[q]
            late_y(q).wait_recv()
            pair[q, :rows] = x_sum[q, :, mine] + y_late[q]

            @pl.when(q != group)
            def _():
                along_z(q).start()

        @pl.when(t == 6)
        def _():
            def take(p, total):
                q = peer(group, p, groups)
                remote(t_z.at[q], t_z.at[q], stz.at[q], rtz.at[q], {"mem": 2 * q + parity}).wait_recv()
                return total + t_z[q]

            final_s[...] = lax.fori_loop(1, groups, take, t_xsum[cut(group, extra)])
            gather_s[slot] = final_s[...]

            def send(p, inner):
                small_gather(peer(me, members - p, members)).start()
                return inner

            lax.fori_loop(1, members, send, 0)

        return carry

    lax.fori_loop(0, max(groups, 4) + 4, step, 0)

    def weights(at, who, where):
        return remote(gather_w.at[at], gather_w.at[at], sgw.at[who], rgw.at[at], where)

    def smalls(at, who, where):
        return remote(gather_b.at[at], gather_b.at[at], sgb.at[who], rgb.at[at], where)

    far = (1 - high) * 2 + low
    near_by = high * 2 + 1 - low
    near_far = (1 - high) * 2 + 1 - low

    def take_small(p, carry):
        k = peer(me, p, members)
        at = slot_of(k)
        remote(gather_s.at[at], gather_s.at[at], stg.at[k], rtg.at[k], {"mem": k}).wait_recv()
        return carry

    lax.fori_loop(1, members, take_small, 0)
    gather_b[band] = gather_s[...]
    smalls(band, 0, across).start()
    smalls(band, 1, partner).start()

    def take_z(p, total):
        q = peer(group, groups - p, groups)
        remote(z_in.at[q], z_in.at[q], sz.at[q], rz.at[q], {"mem": 2 * q + parity}).wait_recv()
        return total + z_in[q]

    gather_w[band] = lax.fori_loop(1, groups, take_z, pair[group])
    weights(band, 0, across).start()
    weights(band, 1, partner).start()
    smalls(far, 2, across).wait_recv()
    smalls(far, 2, partner).start()
    weights(far, 2, across).wait_recv()
    weights(far, 2, partner).start()
    for at in (near_by, near_far):
        smalls(at, 0, partner).wait_recv()
        weights(at, 0, partner).wait_recv()
    for k in range(bands):
        lanes = slice((k % 2) * half + (k // 2) * part, (k % 2) * half + (k // 2) * part + part)
        first_out[:, lanes] = gather_w[k, :rows]
        second_out[:, lanes] = gather_w[k, rows:]
        small_all[:, lanes] = gather_b[k].reshape(small_all.shape[0], part)
    for at, who, where in ((band, 0, across), (band, 1, partner), (far, 2, partner)):
        weights(at, who, where).wait_send()
        smalls(at, who, where).wait_send()
    small_core.wait_send()
    small_y.wait_send()
    small_x.wait_send()

    def drain(k, carry):
        @pl.when(k != me)
        def _():
            small_gather(k).wait_send()

        return carry

    def drain_groups(q, carry):
        core(0, q).wait_send()
        core(1, q).wait_send()
        along_y(q).wait_send()
        along_x(q).wait_send()
        wide_x(q).wait_send()
        late_y(q).wait_send()

        @pl.when(q != group)
        def _():
            along_z(q).wait_send()
            small_z(q).wait_send()

        return carry

    lax.fori_loop(0, members, drain, 0)
    lax.fori_loop(0, groups, drain_groups, 0)


def reduce_scratch(members, bands, features, hidden, extra):
    groups, rows, half, part = members // 2, features // members, hidden // 2, hidden // bands
    dma = pltpu.SemaphoreType.DMA
    height = members * extra
    shapes = [
        (2, features, half), (2, features, half), (features, part), (features, part),
        (groups, rows, half), (groups, rows, half), (groups, rows, part), (groups, rows, part),
        (groups, 2 * rows, part), (groups, 2 * rows, part), (bands, 2 * rows, part),
        (height, half), (height, half), (height, part), (height, part),
        (height // 2, part), (height // 2, part), (groups, extra, part),
        (extra, part), (members, extra, part), (bands, members, extra, part),
    ]
    counts = (
        [(2, groups)] * 2 + [(groups,)] * 10 + [(3,)] * 2 + [(groups,)] * 2 + [(members,)] * 2 + [(bands,)] * 4
    )
    return [pltpu.VMEM(o, jnp.float32) for o in shapes] + [dma(n) for n in counts]


def score_kernel(
    members, bands, chunks, cols, edge,
    latent_ref, first_hbm, first_bias_hbm, second_hbm, second_bias_hbm, out_weight_hbm, out_bias_hbm,
    truth_hbm, node_hbm,
    score_out, first_out, first_bias_out, second_out, second_bias_out, out_weight_out, out_bias_out,
    first_ref, first_bias_ref, second_ref, second_bias_ref, out_weight_ref, out_bias_ref, truth_in, node_ref, inputs_sem,
    rows_in, first_act, first_slope, second_act, second_slope, first_sum, second_sum, small_sum, bias_sum, raw_ref,
    before, after, grad_before, grad_after, sent, ensemble, grads, returned, back,
    halo_send, halo_recv, ghalo_send, ghalo_recv, fwd_send, fwd_recv, ret_send, ret_recv, load,
    score_ref, weight_ref, truth_ref, bias_column, small_all, *reduce_refs,
):
    me = lax.axis_index("mem")
    band = lax.axis_index("band")
    length = raw_ref.shape[2]
    lat_rows = node_ref.shape[0]
    blocks = chunks * members
    taps = stencil_taps(RADIUS)
    has_prev = band > 0
    has_next = band < bands - 1
    prev, following = jnp.maximum(band - 1, 0), jnp.minimum(band + 1, bands - 1)

    def outward(s):
        p = lax.rem(s, members)
        far = members - 1 - p // 2
        return peer(me, jnp.where(lax.rem(p, 2) == 0, far, far - members // 2), members)

    def inward(s):
        return outward(lax.rem(s, members) + members - 1)

    def block_of(s, k):
        return (s // members) * members + k

    def fetch(s):
        chunk, k = s // members, outward(s)
        where = pl.ds(pl.multiple_of((k * chunks + chunk) * cols, cols), cols)
        b = block_of(s, k)
        return pltpu.make_async_copy(latent_ref.at[:, where, :], rows_in.at[b], load.at[b])

    def prefetch(s, carry):
        fetch(s).start()
        return carry

    barrier = pltpu.get_barrier_semaphore()

    def greet(p, carry):
        pl.semaphore_signal(barrier, inc=1, device_id={"mem": peer(me, members - p, members)}, device_id_type=MESH)
        return carry

    lax.fori_loop(1, members, greet, 0)

    for d in range(1, bands):
        pl.semaphore_signal(barrier, inc=1, device_id={"band": lax.rem(band + d, bands)}, device_id_type=MESH)

    pairs = (
        (first_hbm, first_ref), (first_bias_hbm, first_bias_ref), (second_hbm, second_ref),
        (second_bias_hbm, second_bias_ref), (out_weight_hbm, out_weight_ref), (out_bias_hbm, out_bias_ref),
        (truth_hbm, truth_in), (node_hbm, node_ref),
    )
    loads = [pltpu.make_async_copy(source, target, inputs_sem.at[i]) for i, (source, target) in enumerate(pairs)]
    for copy in loads[:2]:
        copy.start()
    fetch(0).start()
    for copy in loads[2:6]:
        copy.start()
    lax.fori_loop(1, blocks, prefetch, 0)
    for copy in loads[6:]:
        copy.start()
    channels, hidden = out_weight_ref.shape
    @pl.when(band == 0)
    def _():
        before[...] = jnp.zeros_like(before)
        grad_before[...] = jnp.zeros_like(grad_before)

    @pl.when(band == bands - 1)
    def _():
        after[...] = jnp.zeros_like(after)
        grad_after[...] = jnp.zeros_like(grad_after)

    def to_next(source, target, b, send, recv):
        return remote(source.at[b, :, pl.ds(length - edge, edge)], target.at[b], send.at[0, b], recv.at[0, b], {"band": following})

    def to_prev(source, target, b, send, recv):
        return remote(source.at[b, :, pl.ds(0, edge)], target.at[b], send.at[1, b], recv.at[1, b], {"band": prev})

    def start_edges(source, low, high, b, send, recv):
        @pl.when(has_next)
        def _():
            to_next(source, low, b, send, recv).start()

        @pl.when(has_prev)
        def _():
            to_prev(source, high, b, send, recv).start()

    def wait_edges(source, low, high, b, send, recv):
        @pl.when(has_prev)
        def _():
            to_next(source, low, b, send, recv).wait_recv()

        @pl.when(has_next)
        def _():
            to_prev(source, high, b, send, recv).wait_recv()

    def drain_edges(source, low, high, b, send, recv):
        @pl.when(has_next)
        def _():
            to_next(source, low, b, send, recv).wait_send()

        @pl.when(has_prev)
        def _():
            to_prev(source, high, b, send, recv).wait_send()

    raw_edges = (raw_ref, before, after)
    grad_edges = (grads, grad_before, grad_after)

    def forward(s, k):
        b = block_of(s, k)
        return remote(sent.at[b], ensemble.at[block_of(s, me)], fwd_send.at[b], fwd_recv.at[block_of(s, me)], {"mem": k})

    def returning(s, k):
        b = block_of(s, k)
        return remote(returned.at[b], back.at[block_of(s, me)], ret_send.at[b], ret_recv.at[block_of(s, me)], {"mem": k})

    def arrived(buffer, sems, s, k):
        b = block_of(s, k)
        remote(buffer.at[b], buffer.at[b], sems.at[b], sems.at[b], {"mem": k}).wait_recv()

    def decode(s):
        b = block_of(s, outward(s))
        fetch(s).wait()
        inputs = rows_in[b].reshape(length, rows_in.shape[3])
        pre = jnp.dot(inputs, first_ref[...], preferred_element_type=jnp.float32) + first_bias_ref[...]
        act, slope = gelu_pair(pre)
        first_act[b] = act.astype(jnp.bfloat16)
        first_slope[b] = slope
        pre = jnp.dot(first_act[b], second_ref[...], preferred_element_type=jnp.float32) + second_bias_ref[...]
        act, slope = gelu_pair(pre)
        second_act[b] = act.astype(jnp.bfloat16)
        second_slope[b] = slope
        raw_ref[b] = contract(out_weight_ref[...], second_act[b], 1, 1) + bias_column[...]

    def decode_edges(s):
        start_edges(*raw_edges, block_of(s, outward(s)), halo_send, halo_recv)

    def spread(s):
        k = outward(s)
        b = block_of(s, k)
        wait_edges(*raw_edges, b, halo_send, halo_recv)
        smooth = smooth_block(before[b], raw_ref[b], after[b], taps, cols)

        @pl.when(k != me)
        def _():
            sent[b] = smooth
            forward(s, k).start()

        @pl.when(k == me)
        def _():
            ensemble[b] = smooth

    lead = 2

    def early_step(s, carry):
        decode(s)
        return carry

    def early_edges(s, carry):
        decode_edges(s)
        return carry

    def forward_step(s, carry):
        @pl.when(s < blocks)
        def _():
            decode(s)
            decode_edges(s)

        spread(s - lead)
        return carry

    for copy in loads[:6]:
        copy.wait()
    shape = (channels, channels)
    diagonal = lax.broadcasted_iota(jnp.int32, shape, 0) == lax.broadcasted_iota(jnp.int32, shape, 1)
    bias_column[...] = jnp.sum(jnp.where(diagonal, out_bias_ref[...], 0.0), axis=1, keepdims=True)
    lax.fori_loop(0, lead, early_step, 0)
    pl.semaphore_wait(barrier, members + bands - 2)
    lax.fori_loop(0, lead, early_edges, 0)
    lax.fori_loop(lead, blocks + lead, forward_step, 0)
    for copy in loads[6:]:
        copy.wait()
    for c in range(chunks):
        truth_ref[c] = truth_in[:, c * cols : (c + 1) * cols, :].reshape(length, channels).T
        for row in range(lat_rows):
            weight_ref[c, :, row * cols : (row + 1) * cols] = node_ref[row : row + 1, c * cols : (c + 1) * cols]
    first_sum[...] = jnp.zeros_like(first_sum)
    second_sum[...] = jnp.zeros_like(second_sum)
    small_sum[...] = jnp.zeros_like(small_sum)
    bias_sum[...] = jnp.zeros_like(bias_sum)
    score_ref[...] = jnp.zeros_like(score_ref)
    pair_count = members * (members - 1)
    row_ids = lax.broadcasted_iota(jnp.int32, (members, LANES), 0)

    def score_chunk(c, carry):
        start = c * members

        def collect(p, inner):
            arrived(ensemble, fwd_recv, start, peer(me, p, members))
            return inner

        lax.fori_loop(1, members, collect, 0)

        def member(p, inner):
            m = outward(p)
            b = start + m

            def piece(i, innermost):
                lanes = pl.ds(pl.multiple_of(i * LANES, LANES), LANES)
                mine = ensemble[b, :, lanes]
                gaps = mine[None] - ensemble[pl.ds(start, members), :, lanes]
                distance = jnp.sqrt(jnp.sum(gaps * gaps, axis=1) + epsilon)
                own = row_ids == m
                inverse = jnp.where(own, 0.0, 1.0 / distance)
                spread_sum = jnp.sum(jnp.where(own, 0.0, distance), axis=0, keepdims=True)
                pair_grad = jnp.sum(gaps * inverse[:, None, :], axis=0)
                error = mine - truth_ref[c, :, lanes]
                skill = jnp.sqrt(jnp.sum(error * error, axis=0, keepdims=True) + epsilon)
                score_ref[c, :, lanes] += skill / members - spread_sum / (2.0 * pair_count)
                grads[b, :, lanes] = weight_ref[c, :, lanes] * (error / (members * skill) - pair_grad / pair_count)
                return innermost

            lax.fori_loop(0, length // LANES, piece, 0)
            start_edges(*grad_edges, b, ghalo_send, ghalo_recv)
            return inner

        lax.fori_loop(0, members, member, 0)

        def give(p, inner):
            m = outward(p)
            b = start + m
            wait_edges(*grad_edges, b, ghalo_send, ghalo_recv)
            smooth = smooth_block(grad_before[b], grads[b], grad_after[b], taps, cols)

            @pl.when(m != me)
            def _():
                returned[b] = smooth
                returning(start, m).start()

            @pl.when(m == me)
            def _():
                back[b] = smooth

            return inner

        lax.fori_loop(0, members, give, 0)
        return carry

    lax.fori_loop(0, chunks, score_chunk, 0)

    def finish(s, carry):
        k = inward(s)
        b = block_of(s, k)

        @pl.when(k != me)
        def _():
            arrived(back, ret_recv, s, k)

        grad_raw = back[b]
        grad_low = grad_raw.astype(jnp.bfloat16)
        bias_sum[...] += jnp.sum(grad_raw, axis=1, keepdims=True)
        small_sum[:channels] += jnp.dot(grad_low, second_act[b], preferred_element_type=jnp.float32)
        delta = contract(grad_low, out_weight_ref[...], 0, 0) * second_slope[b]
        small_sum[channels + 1 : channels + 2] += jnp.sum(delta, axis=0, keepdims=True)
        low = delta.astype(jnp.bfloat16)
        second_sum[...] += contract(first_act[b], low, 0, 0)
        delta = contract(low, second_ref[...], 1, 1) * first_slope[b]
        small_sum[channels : channels + 1] += jnp.sum(delta, axis=0, keepdims=True)
        inputs = rows_in[b].reshape(length, rows_in.shape[3])
        first_sum[...] += contract(inputs, delta.astype(jnp.bfloat16), 0, 0)
        return carry

    lax.fori_loop(0, blocks, finish, 0)
    small_sum[channels + 2 : channels + 3, :channels] = jnp.sum(
        jnp.where(diagonal, bias_sum[...], 0.0), axis=0, keepdims=True
    )
    reduce_in_kernel(
        members, bands, first_sum, second_sum, small_sum, first_out, second_out, small_all, *reduce_refs
    )
    for c in range(chunks):
        for row in range(lat_rows):
            score_out[row : row + 1, c * cols : (c + 1) * cols] = score_ref[c, :, row * cols : (row + 1) * cols]
    out_weight_out[...] = small_all[:channels]
    first_bias_out[...] = small_all[channels : channels + 1]
    second_bias_out[...] = small_all[channels + 1 : channels + 2]
    out_bias_out[...] = small_all[channels + 2 : channels + 3, :channels]

    def drain(s, carry):
        k = inward(s)
        b = block_of(s, k)
        drain_edges(*raw_edges, b, halo_send, halo_recv)
        drain_edges(*grad_edges, b, ghalo_send, ghalo_recv)

        @pl.when(k != me)
        def _():
            forward(s, k).wait_send()
            returning(s, k).wait_send()

        return carry

    lax.fori_loop(0, blocks, drain, 0)


def score_and_gradient(latent, weights, truth, weight, members, bands, cols, rows, extra):
    lat_rows, _, features = latent.shape
    channels = truth.shape[2]
    hidden = weights[0].shape[1]
    chunks = 2 if cols % 32 == 0 and lat_rows * cols % (2 * LANES) == 0 else 1
    part_cols = cols // chunks
    length = lat_rows * part_cols
    edge = min(length, -(-RADIUS * part_cols // LANES) * LANES)
    blocks = chunks * members
    block = (blocks, channels, length)
    halo = (blocks, channels, edge)
    units = (blocks, length, hidden)
    dma = pltpu.SemaphoreType.DMA
    vmem = pl.BlockSpec(memory_space=pltpu.VMEM)
    single, half = jnp.float32, jnp.bfloat16
    return pl.pallas_call(
        functools.partial(score_kernel, members, bands, chunks, part_cols, edge),
        out_shape=tuple(
            jax.ShapeDtypeStruct(o, single)
            for o in (
                (lat_rows, cols), (rows, hidden), (1, hidden), (rows, hidden), (1, hidden),
                (channels, hidden), (1, channels),
            )
        ),
        in_specs=[pl.BlockSpec(memory_space=pl.ANY)] * 9,
        out_specs=(vmem,) * 7,
        scratch_shapes=[pltpu.VMEM(v.shape, v.dtype) for v in (*weights, truth, weight)]
        + [dma((8,))]
        + [
            pltpu.VMEM((blocks, lat_rows, part_cols, features), half),
            pltpu.VMEM(units, half), pltpu.VMEM(units, single),
            pltpu.VMEM(units, half), pltpu.VMEM(units, single),
            pltpu.VMEM((features, hidden), single), pltpu.VMEM((hidden, hidden), single),
            pltpu.VMEM((members * extra, hidden), single), pltpu.VMEM((channels, 1), single),
            pltpu.VMEM(block, single),
        ]
        + [pltpu.VMEM(halo, single)] * 4
        + [pltpu.VMEM(block, single)] * 5
        + [dma((2, blocks))] * 4
        + [dma((blocks,))] * 5
        + [pltpu.VMEM(o, single) for o in [
            (chunks, 1, length), (chunks, 1, length), (chunks, channels, length), (channels, 1),
            (members * extra, hidden),
        ]]
        + reduce_scratch(members, bands, features, hidden, extra),
        compiler_params=pltpu.CompilerParams(collective_id=0, has_side_effects=True, vmem_limit_bytes=60 << 20),
    )(latent, *weights, truth, weight)


def write_kernel(*refs):
    count = len(refs) // 2
    for source, target in zip(refs[:count], refs[count:]):
        target[...] = source[...]


def write_results(values):
    vmem = pl.BlockSpec(memory_space=pltpu.VMEM)
    return pl.pallas_call(
        write_kernel,
        out_shape=tuple(jax.ShapeDtypeStruct(v.shape, v.dtype) for v in values),
        in_specs=[vmem] * len(values),
        out_specs=(vmem,) * len(values),
    )(*values)


def body(
    latent, truth, node_weight, first_weight, first_bias, second_weight, second_bias, out_weight, out_bias
):
    members, bands = lax.axis_size("mem"), lax.axis_size("band")
    _, lat_rows, lon_cols, features = latent.shape
    channels, hidden = out_weight.shape
    cols = lon_cols // members
    rows = features // members
    extra = -(-(channels + 3) // (8 * members)) * 8
    weights = (
        first_weight, first_bias[None], second_weight, second_bias[None], out_weight, out_bias[None]
    )
    score, first, first_b, second, second_b, out_w, out_b = write_results(score_and_gradient(
        latent.reshape(lat_rows, lon_cols, features), weights,
        jnp.transpose(truth, (1, 2, 0)), node_weight, members, bands, cols, rows, extra,
    ))
    return (score, first, first_b[0], second, second_b[0], out_w, out_b[0])


def solution(mesh):
    in_specs = (
        P("mem", "band", None, None),
        P(None, "band", "mem"),
        P("band", "mem"),
        P(),
        P(),
        P(),
        P(),
        P(),
        P(),
    )
    out_specs = (P("band", "mem"), P("mem", None), P(), P("mem", None), P(), P(), P())
    return jax.shard_map(body, mesh=mesh, in_specs=in_specs, out_specs=out_specs, check_vma=False)
```

```python
import functools
import math
import jax
import jax.numpy as jnp
from jax import lax
from jax.experimental import pallas as pl
from jax.experimental.pallas import tpu as pltpu
from jax.sharding import PartitionSpec as P

RADIUS = 3
LANES = 128
MESH = pl.DeviceIdType.MESH

root_half = 0.7071067811865476
density_scale = 0.3989422804014327
tap_spread = 1.5
epsilon = 1e-06


def gelu_pair(value):
    normal_cdf = 0.5 * (1.0 + lax.erf(value * root_half))
    return (value * normal_cdf, normal_cdf + value * jnp.exp(-0.5 * value * value) * density_scale)


def stencil_taps(radius):
    weights = [math.exp(-k * k / (2.0 * tap_spread * tap_spread)) for k in range(-radius, radius + 1)]
    return [w / sum(weights) for w in weights]


def remote(src, dst, send, recv, where):
    return pltpu.make_async_remote_copy(
        src_ref=src, dst_ref=dst, send_sem=send, recv_sem=recv, device_id=where, device_id_type=MESH
    )


def peer(me, p, count):
    if count & (count - 1):
        return lax.rem(me + p, count)
    total, bit = 0, 1
    while bit < count:
        total = total + lax.rem(me // bit + p // bit, 2) * bit
        bit *= 2
    return total


def smooth_block(before, own, after, taps, cols):
    edge, length = before.shape[1], own.shape[1]
    padded = jnp.concatenate([before, own, after], axis=1)
    width = padded.shape[1]
    rolled = {0: padded}
    total = None
    for index, tap in enumerate(taps):
        shift = (index - RADIUS) * cols
        rest = shift % LANES
        if rest not in rolled:
            rolled[rest] = pltpu.roll(padded, width - rest, 1)
        start = edge + shift - rest
        term = tap * rolled[rest][:, start : start + length]
        total = term if total is None else total + term
    return total


def contract(left, right, left_dim, right_dim):
    return lax.dot_general(
        left, right, (((left_dim,), (right_dim,)), ((), ())), preferred_element_type=jnp.float32
    )


def reduce_in_kernel(
    members, bands, first_sum, second_sum, small_sum, first_out, second_out, small_all,
    core_in, held, y_in, y_sum, x_wide, x_sum, x_in, y_late, pair, z_in, gather_w,
    t_core, t_held, t_y, t_ysum, t_x, t_xsum, t_z, final_s, gather_s, gather_b,
    sc, rc, sy, ry, sx, rx, sxw, rxw, syl, ryl, sz, rz, st, rt, stz, rtz, stg, rtg, sgw, rgw, sgb, rgb,
):
    me = lax.axis_index("mem")
    band = lax.axis_index("band")
    low, high = lax.rem(band, 2), band // 2
    parity, group = lax.rem(me, 2), me // 2
    groups = members // 2
    rows = first_out.shape[0]
    hidden = first_sum.shape[1]
    half, part = hidden // 2, hidden // bands
    extra = final_s.shape[0]
    partner = {"band": high * 2 + 1 - low}
    across = {"band": (1 - high) * 2 + low}
    beside = {"mem": me + 1 - 2 * parity}

    def cut(index, size):
        return pl.ds(pl.multiple_of(index * size, size), size)

    mine, other = cut(high, part), cut(1 - high, part)

    def both(q):
        return cut(q, 2 * rows)

    def kept(q):
        return cut(2 * q + parity, rows)

    def given(q):
        return cut(2 * q + 1 - parity, rows)

    def core(w, q):
        source = (second_sum, first_sum)[w]
        return remote(
            source.at[both(q), cut(1 - low, half)], core_in.at[w, both(q)], sc.at[w, q], rc.at[w, q], partner
        )

    def along_y(q):
        return remote(held.at[0, both(q), other], y_in.at[both(q)], sy.at[q], ry.at[q], across)

    def along_x(q):
        return remote(y_sum.at[given(q)], x_in.at[q], sx.at[q], rx.at[q], beside)

    def wide_x(q):
        return remote(held.at[1, given(q)], x_wide.at[q], sxw.at[q], rxw.at[q], beside)

    def late_y(q):
        return remote(x_sum.at[q, :, other], y_late.at[q], syl.at[q], ryl.at[q], across)

    def along_z(q):
        return remote(pair.at[q], z_in.at[group], sz.at[q], rz.at[group], {"mem": 2 * q + parity})

    small_core = remote(small_sum.at[:, cut(1 - low, half)], t_core, st.at[0], rt.at[0], partner)
    small_y = remote(t_held.at[:, other], t_y, st.at[1], rt.at[1], across)
    spread = groups * extra
    small_x = remote(t_ysum.at[cut(1 - parity, spread)], t_x, st.at[2], rt.at[2], beside)
    slot = parity * groups + group

    def small_z(q):
        return remote(t_xsum.at[cut(q, extra)], t_z.at[group], stz.at[q], rtz.at[group], {"mem": 2 * q + parity})

    def slot_of(k):
        return lax.rem(k, 2) * groups + k // 2

    def small_gather(k):
        return remote(final_s, gather_s.at[slot], stg.at[k], rtg.at[me], {"mem": k})

    def step_core(t, carry):
        q = peer(group, groups - 1 - t, groups)
        core(0, q).start()
        core(1, q).start()
        return carry

    small_core.start()
    lax.fori_loop(0, groups, step_core, 0)
    small_core.wait_recv()
    t_held[...] = small_sum[:, cut(low, half)] + t_core[...]
    small_y.start()

    def near(index):
        return peer(group, groups - 1 - index, groups)

    def step(t, carry):
        @pl.when(t < groups)
        def _():
            q = near(t)
            core(0, q).wait_recv()
            held[0, both(q)] = second_sum[both(q), cut(low, half)] + core_in[0, both(q)]
            along_y(q).start()
            core(1, q).wait_recv()
            held[1, both(q)] = first_sum[both(q), cut(low, half)] + core_in[1, both(q)]
            wide_x(q).start()

        @pl.when(t == 2)
        def _():
            small_y.wait_recv()
            t_ysum[...] = t_held[:, mine] + t_y[...]
            small_x.start()

        @pl.when((t >= 2) & (t < groups + 2))
        def _():
            q = near(t - 2)
            along_y(q).wait_recv()
            y_sum[both(q)] = held[0, both(q), mine] + y_in[both(q)]
            along_x(q).start()
            wide_x(q).wait_recv()
            x_sum[q] = held[1, kept(q)] + x_wide[q]
            late_y(q).start()

        @pl.when(t == 3)
        def _():
            small_x.wait_recv()
            t_xsum[...] = t_ysum[cut(parity, spread)] + t_x[...]

            def send(p, inner):
                small_z(peer(group, groups - p, groups)).start()
                return inner

            lax.fori_loop(1, groups, send, 0)

        @pl.when((t >= 4) & (t < groups + 4))
        def _():
            q = near(t - 4)
            along_x(q).wait_recv()
            pair[q, rows:] = y_sum[kept(q)] + x_in[q]
            late_y(q).wait_recv()
            pair[q, :rows] = x_sum[q, :, mine] + y_late[q]

            @pl.when(q != group)
            def _():
                along_z(q).start()

        @pl.when(t == 4)
        def _():
            def take(p, total):
                q = peer(group, p, groups)
                remote(t_z.at[q], t_z.at[q], stz.at[q], rtz.at[q], {"mem": 2 * q + parity}).wait_recv()
                return total + t_z[q]

            final_s[...] = lax.fori_loop(1, groups, take, t_xsum[cut(group, extra)])
            gather_s[slot] = final_s[...]

            def send(p, inner):
                small_gather(peer(me, members - p, members)).start()
                return inner

            lax.fori_loop(1, members, send, 0)

        return carry

    lax.fori_loop(0, max(groups, 4) + 4, step, 0)

    def weights(at, who, where):
        return remote(gather_w.at[at], gather_w.at[at], sgw.at[who], rgw.at[at], where)

    def smalls(at, who, where):
        return remote(gather_b.at[at], gather_b.at[at], sgb.at[who], rgb.at[at], where)

    far = (1 - high) * 2 + low
    near_by = high * 2 + 1 - low
    near_far = (1 - high) * 2 + 1 - low

    def take_small(p, carry):
        k = peer(me, p, members)
        at = slot_of(k)
        remote(gather_s.at[at], gather_s.at[at], stg.at[k], rtg.at[k], {"mem": k}).wait_recv()
        return carry

    lax.fori_loop(1, members, take_small, 0)
    gather_b[band] = gather_s[...]
    smalls(band, 0, across).start()
    smalls(band, 1, partner).start()

    def take_z(p, total):
        q = peer(group, groups - p, groups)
        remote(z_in.at[q], z_in.at[q], sz.at[q], rz.at[q], {"mem": 2 * q + parity}).wait_recv()
        return total + z_in[q]

    gather_w[band] = lax.fori_loop(1, groups, take_z, pair[group])
    weights(band, 0, across).start()
    weights(band, 1, partner).start()
    smalls(far, 2, across).wait_recv()
    smalls(far, 2, partner).start()
    weights(far, 2, across).wait_recv()
    weights(far, 2, partner).start()
    for at in (near_by, near_far):
        smalls(at, 0, partner).wait_recv()
        weights(at, 0, partner).wait_recv()
    for k in range(bands):
        lanes = slice((k % 2) * half + (k // 2) * part, (k % 2) * half + (k // 2) * part + part)
        first_out[:, lanes] = gather_w[k, :rows]
        second_out[:, lanes] = gather_w[k, rows:]
        small_all[:, lanes] = gather_b[k].reshape(small_all.shape[0], part)
    for at, who, where in ((band, 0, across), (band, 1, partner), (far, 2, partner)):
        weights(at, who, where).wait_send()
        smalls(at, who, where).wait_send()
    small_core.wait_send()
    small_y.wait_send()
    small_x.wait_send()

    def drain(k, carry):
        @pl.when(k != me)
        def _():
            small_gather(k).wait_send()

        return carry

    def drain_groups(q, carry):
        core(0, q).wait_send()
        core(1, q).wait_send()
        along_y(q).wait_send()
        along_x(q).wait_send()
        wide_x(q).wait_send()
        late_y(q).wait_send()

        @pl.when(q != group)
        def _():
            along_z(q).wait_send()
            small_z(q).wait_send()

        return carry

    lax.fori_loop(0, members, drain, 0)
    lax.fori_loop(0, groups, drain_groups, 0)


def reduce_scratch(members, bands, features, hidden, extra):
    groups, rows, half, part = members // 2, features // members, hidden // 2, hidden // bands
    dma = pltpu.SemaphoreType.DMA
    height = members * extra
    shapes = [
        (2, features, half), (2, features, half), (features, part), (features, part),
        (groups, rows, half), (groups, rows, half), (groups, rows, part), (groups, rows, part),
        (groups, 2 * rows, part), (groups, 2 * rows, part), (bands, 2 * rows, part),
        (height, half), (height, half), (height, part), (height, part),
        (height // 2, part), (height // 2, part), (groups, extra, part),
        (extra, part), (members, extra, part), (bands, members, extra, part),
    ]
    counts = (
        [(2, groups)] * 2 + [(groups,)] * 10 + [(3,)] * 2 + [(groups,)] * 2 + [(members,)] * 2 + [(bands,)] * 4
    )
    return [pltpu.VMEM(o, jnp.float32) for o in shapes] + [dma(n) for n in counts]


def score_kernel(
    members, bands, chunks, cols, edge,
    latent_ref, first_hbm, first_bias_hbm, second_hbm, second_bias_hbm, out_weight_hbm, out_bias_hbm,
    truth_hbm, node_hbm,
    score_out, first_out, first_bias_out, second_out, second_bias_out, out_weight_out, out_bias_out,
    first_ref, first_bias_ref, second_ref, second_bias_ref, out_weight_ref, out_bias_ref, truth_in, node_ref, inputs_sem,
    rows_in, first_act, first_slope, second_act, second_slope, first_sum, second_sum, small_sum, bias_sum, raw_ref,
    before, after, grad_before, grad_after, sent, ensemble, grads, returned, back,
    halo_send, halo_recv, ghalo_send, ghalo_recv, fwd_send, fwd_recv, ret_send, ret_recv, load,
    score_ref, weight_ref, truth_ref, bias_column, small_all, *reduce_refs,
):
    me = lax.axis_index("mem")
    band = lax.axis_index("band")
    length = raw_ref.shape[2]
    lat_rows = node_ref.shape[0]
    blocks = chunks * members
    taps = stencil_taps(RADIUS)
    has_prev = band > 0
    has_next = band < bands - 1
    prev, following = jnp.maximum(band - 1, 0), jnp.minimum(band + 1, bands - 1)

    def outward(s):
        p = lax.rem(s, members)
        far = members - 1 - p // 2
        return peer(me, jnp.where(lax.rem(p, 2) == 0, far, far - members // 2), members)

    def inward(s):
        return outward(lax.rem(s, members) + members - 1)

    def block_of(s, k):
        return (s // members) * members + k

    def fetch(s):
        chunk, k = s // members, outward(s)
        where = pl.ds(pl.multiple_of((k * chunks + chunk) * cols, cols), cols)
        b = block_of(s, k)
        return pltpu.make_async_copy(latent_ref.at[:, where, :], rows_in.at[b], load.at[b])

    def prefetch(s, carry):
        fetch(s).start()
        return carry

    barrier = pltpu.get_barrier_semaphore()

    def greet(p, carry):
        pl.semaphore_signal(barrier, inc=1, device_id={"mem": peer(me, members - p, members)}, device_id_type=MESH)
        return carry

    lax.fori_loop(1, members, greet, 0)

    for d in range(1, bands):
        pl.semaphore_signal(barrier, inc=1, device_id={"band": lax.rem(band + d, bands)}, device_id_type=MESH)

    pairs = (
        (first_hbm, first_ref), (first_bias_hbm, first_bias_ref), (second_hbm, second_ref),
        (second_bias_hbm, second_bias_ref), (out_weight_hbm, out_weight_ref), (out_bias_hbm, out_bias_ref),
        (truth_hbm, truth_in), (node_hbm, node_ref),
    )
    loads = [pltpu.make_async_copy(source, target, inputs_sem.at[i]) for i, (source, target) in enumerate(pairs)]
    for copy in loads[:2]:
        copy.start()
    fetch(0).start()
    for copy in loads[2:6]:
        copy.start()
    lax.fori_loop(1, blocks, prefetch, 0)
    for copy in loads[6:]:
        copy.start()
    channels, hidden = out_weight_ref.shape
    @pl.when(band == 0)
    def _():
        before[...] = jnp.zeros_like(before)
        grad_before[...] = jnp.zeros_like(grad_before)

    @pl.when(band == bands - 1)
    def _():
        after[...] = jnp.zeros_like(after)
        grad_after[...] = jnp.zeros_like(grad_after)

    def to_next(source, target, b, send, recv):
        return remote(source.at[b, :, pl.ds(length - edge, edge)], target.at[b], send.at[0, b], recv.at[0, b], {"band": following})

    def to_prev(source, target, b, send, recv):
        return remote(source.at[b, :, pl.ds(0, edge)], target.at[b], send.at[1, b], recv.at[1, b], {"band": prev})

    def start_edges(source, low, high, b, send, recv):
        @pl.when(has_next)
        def _():
            to_next(source, low, b, send, recv).start()

        @pl.when(has_prev)
        def _():
            to_prev(source, high, b, send, recv).start()

    def wait_edges(source, low, high, b, send, recv):
        @pl.when(has_prev)
        def _():
            to_next(source, low, b, send, recv).wait_recv()

        @pl.when(has_next)
        def _():
            to_prev(source, high, b, send, recv).wait_recv()

    def drain_edges(source, low, high, b, send, recv):
        @pl.when(has_next)
        def _():
            to_next(source, low, b, send, recv).wait_send()

        @pl.when(has_prev)
        def _():
            to_prev(source, high, b, send, recv).wait_send()

    raw_edges = (raw_ref, before, after)
    grad_edges = (grads, grad_before, grad_after)

    def forward(s, k):
        b = block_of(s, k)
        return remote(sent.at[b], ensemble.at[block_of(s, me)], fwd_send.at[b], fwd_recv.at[block_of(s, me)], {"mem": k})

    def returning(s, k):
        b = block_of(s, k)
        return remote(returned.at[b], back.at[block_of(s, me)], ret_send.at[b], ret_recv.at[block_of(s, me)], {"mem": k})

    def arrived(buffer, sems, s, k):
        b = block_of(s, k)
        remote(buffer.at[b], buffer.at[b], sems.at[b], sems.at[b], {"mem": k}).wait_recv()

    def decode(s):
        b = block_of(s, outward(s))
        fetch(s).wait()
        inputs = rows_in[b].reshape(length, rows_in.shape[3])
        pre = jnp.dot(inputs, first_ref[...], preferred_element_type=jnp.float32) + first_bias_ref[...]
        act, slope = gelu_pair(pre)
        first_act[b] = act.astype(jnp.bfloat16)
        first_slope[b] = slope
        pre = jnp.dot(first_act[b], second_ref[...], preferred_element_type=jnp.float32) + second_bias_ref[...]
        act, slope = gelu_pair(pre)
        second_act[b] = act.astype(jnp.bfloat16)
        second_slope[b] = slope
        raw_ref[b] = contract(out_weight_ref[...], second_act[b], 1, 1) + bias_column[...]

    def decode_edges(s):
        start_edges(*raw_edges, block_of(s, outward(s)), halo_send, halo_recv)

    def spread(s):
        k = outward(s)
        b = block_of(s, k)
        wait_edges(*raw_edges, b, halo_send, halo_recv)
        smooth = smooth_block(before[b], raw_ref[b], after[b], taps, cols)

        @pl.when(k != me)
        def _():
            sent[b] = smooth
            forward(s, k).start()

        @pl.when(k == me)
        def _():
            ensemble[b] = smooth

    lead = 2

    def early_step(s, carry):
        decode(s)
        return carry

    def early_edges(s, carry):
        decode_edges(s)
        return carry

    def forward_step(s, carry):
        @pl.when(s < blocks)
        def _():
            decode(s)
            decode_edges(s)

        spread(s - lead)
        return carry

    for copy in loads[:6]:
        copy.wait()
    shape = (channels, channels)
    diagonal = lax.broadcasted_iota(jnp.int32, shape, 0) == lax.broadcasted_iota(jnp.int32, shape, 1)
    bias_column[...] = jnp.sum(jnp.where(diagonal, out_bias_ref[...], 0.0), axis=1, keepdims=True)
    lax.fori_loop(0, lead, early_step, 0)
    pl.semaphore_wait(barrier, members + bands - 2)
    lax.fori_loop(0, lead, early_edges, 0)
    lax.fori_loop(lead, blocks + lead, forward_step, 0)
    for copy in loads[6:]:
        copy.wait()
    for c in range(chunks):
        truth_ref[c] = truth_in[:, c * cols : (c + 1) * cols, :].reshape(length, channels).T
        for row in range(lat_rows):
            weight_ref[c, :, row * cols : (row + 1) * cols] = node_ref[row : row + 1, c * cols : (c + 1) * cols]
    first_sum[...] = jnp.zeros_like(first_sum)
    second_sum[...] = jnp.zeros_like(second_sum)
    small_sum[...] = jnp.zeros_like(small_sum)
    bias_sum[...] = jnp.zeros_like(bias_sum)
    score_ref[...] = jnp.zeros_like(score_ref)
    pair_count = members * (members - 1)
    row_ids = lax.broadcasted_iota(jnp.int32, (members, LANES), 0)

    def score_chunk(c, carry):
        start = c * members

        def collect(p, inner):
            arrived(ensemble, fwd_recv, start, peer(me, p, members))
            return inner

        lax.fori_loop(1, members, collect, 0)

        def member(p, inner):
            m = outward(p)
            b = start + m

            def piece(i, innermost):
                lanes = pl.ds(pl.multiple_of(i * LANES, LANES), LANES)
                mine = ensemble[b, :, lanes]
                gaps = mine[None] - ensemble[pl.ds(start, members), :, lanes]
                distance = jnp.sqrt(jnp.sum(gaps * gaps, axis=1) + epsilon)
                own = row_ids == m
                inverse = jnp.where(own, 0.0, 1.0 / distance)
                spread_sum = jnp.sum(jnp.where(own, 0.0, distance), axis=0, keepdims=True)
                pair_grad = jnp.sum(gaps * inverse[:, None, :], axis=0)
                error = mine - truth_ref[c, :, lanes]
                skill = jnp.sqrt(jnp.sum(error * error, axis=0, keepdims=True) + epsilon)
                score_ref[c, :, lanes] += skill / members - spread_sum / (2.0 * pair_count)
                grads[b, :, lanes] = weight_ref[c, :, lanes] * (error / (members * skill) - pair_grad / pair_count)
                return innermost

            lax.fori_loop(0, length // LANES, piece, 0)
            start_edges(*grad_edges, b, ghalo_send, ghalo_recv)
            return inner

        lax.fori_loop(0, members, member, 0)

        def give(p, inner):
            m = outward(p)
            b = start + m
            wait_edges(*grad_edges, b, ghalo_send, ghalo_recv)
            smooth = smooth_block(grad_before[b], grads[b], grad_after[b], taps, cols)

            @pl.when(m != me)
            def _():
                returned[b] = smooth
                returning(start, m).start()

            @pl.when(m == me)
            def _():
                back[b] = smooth

            return inner

        lax.fori_loop(0, members, give, 0)
        return carry

    lax.fori_loop(0, chunks, score_chunk, 0)

    def finish(s, carry):
        k = inward(s)
        b = block_of(s, k)

        @pl.when(k != me)
        def _():
            arrived(back, ret_recv, s, k)

        grad_raw = back[b]
        grad_low = grad_raw.astype(jnp.bfloat16)
        bias_sum[...] += jnp.sum(grad_raw, axis=1, keepdims=True)
        small_sum[:channels] += jnp.dot(grad_low, second_act[b], preferred_element_type=jnp.float32)
        delta = contract(grad_low, out_weight_ref[...], 0, 0) * second_slope[b]
        small_sum[channels + 1 : channels + 2] += jnp.sum(delta, axis=0, keepdims=True)
        low = delta.astype(jnp.bfloat16)
        second_sum[...] += contract(first_act[b], low, 0, 0)
        delta = contract(low, second_ref[...], 1, 1) * first_slope[b]
        small_sum[channels : channels + 1] += jnp.sum(delta, axis=0, keepdims=True)
        inputs = rows_in[b].reshape(length, rows_in.shape[3])
        first_sum[...] += contract(inputs, delta.astype(jnp.bfloat16), 0, 0)
        return carry

    lax.fori_loop(0, blocks, finish, 0)
    small_sum[channels + 2 : channels + 3, :channels] = jnp.sum(
        jnp.where(diagonal, bias_sum[...], 0.0), axis=0, keepdims=True
    )
    reduce_in_kernel(
        members, bands, first_sum, second_sum, small_sum, first_out, second_out, small_all, *reduce_refs
    )
    for c in range(chunks):
        for row in range(lat_rows):
            score_out[row : row + 1, c * cols : (c + 1) * cols] = score_ref[c, :, row * cols : (row + 1) * cols]
    out_weight_out[...] = small_all[:channels]
    first_bias_out[...] = small_all[channels : channels + 1]
    second_bias_out[...] = small_all[channels + 1 : channels + 2]
    out_bias_out[...] = small_all[channels + 2 : channels + 3, :channels]

    def drain(s, carry):
        k = inward(s)
        b = block_of(s, k)
        drain_edges(*raw_edges, b, halo_send, halo_recv)
        drain_edges(*grad_edges, b, ghalo_send, ghalo_recv)

        @pl.when(k != me)
        def _():
            forward(s, k).wait_send()
            returning(s, k).wait_send()

        return carry

    lax.fori_loop(0, blocks, drain, 0)


def score_and_gradient(latent, weights, truth, weight, members, bands, cols, rows, extra):
    lat_rows, _, features = latent.shape
    channels = truth.shape[2]
    hidden = weights[0].shape[1]
    chunks = 2 if cols % 32 == 0 and lat_rows * cols % (2 * LANES) == 0 else 1
    part_cols = cols // chunks
    length = lat_rows * part_cols
    edge = min(length, -(-RADIUS * part_cols // LANES) * LANES)
    blocks = chunks * members
    block = (blocks, channels, length)
    halo = (blocks, channels, edge)
    units = (blocks, length, hidden)
    dma = pltpu.SemaphoreType.DMA
    vmem = pl.BlockSpec(memory_space=pltpu.VMEM)
    single, half = jnp.float32, jnp.bfloat16
    return pl.pallas_call(
        functools.partial(score_kernel, members, bands, chunks, part_cols, edge),
        out_shape=tuple(
            jax.ShapeDtypeStruct(o, single)
            for o in (
                (lat_rows, cols), (rows, hidden), (1, hidden), (rows, hidden), (1, hidden),
                (channels, hidden), (1, channels),
            )
        ),
        in_specs=[pl.BlockSpec(memory_space=pl.ANY)] * 9,
        out_specs=(vmem,) * 7,
        scratch_shapes=[pltpu.VMEM(v.shape, v.dtype) for v in (*weights, truth, weight)]
        + [dma((8,))]
        + [
            pltpu.VMEM((blocks, lat_rows, part_cols, features), half),
            pltpu.VMEM(units, half), pltpu.VMEM(units, single),
            pltpu.VMEM(units, half), pltpu.VMEM(units, single),
            pltpu.VMEM((features, hidden), single), pltpu.VMEM((hidden, hidden), single),
            pltpu.VMEM((members * extra, hidden), single), pltpu.VMEM((channels, 1), single),
            pltpu.VMEM(block, single),
        ]
        + [pltpu.VMEM(halo, single)] * 4
        + [pltpu.VMEM(block, single)] * 5
        + [dma((2, blocks))] * 4
        + [dma((blocks,))] * 5
        + [pltpu.VMEM(o, single) for o in [
            (chunks, 1, length), (chunks, 1, length), (chunks, channels, length), (channels, 1),
            (members * extra, hidden),
        ]]
        + reduce_scratch(members, bands, features, hidden, extra),
        compiler_params=pltpu.CompilerParams(collective_id=0, has_side_effects=True, vmem_limit_bytes=60 << 20),
    )(latent, *weights, truth, weight)


def write_kernel(*refs):
    count = len(refs) // 2
    for source, target in zip(refs[:count], refs[count:]):
        target[...] = source[...]


def write_results(values):
    vmem = pl.BlockSpec(memory_space=pltpu.VMEM)
    return pl.pallas_call(
        write_kernel,
        out_shape=tuple(jax.ShapeDtypeStruct(v.shape, v.dtype) for v in values),
        in_specs=[vmem] * len(values),
        out_specs=(vmem,) * len(values),
    )(*values)


def body(
    latent, truth, node_weight, first_weight, first_bias, second_weight, second_bias, out_weight, out_bias
):
    members, bands = lax.axis_size("mem"), lax.axis_size("band")
    _, lat_rows, lon_cols, features = latent.shape
    channels, hidden = out_weight.shape
    cols = lon_cols // members
    rows = features // members
    extra = -(-(channels + 3) // (8 * members)) * 8
    weights = (
        first_weight, first_bias[None], second_weight, second_bias[None], out_weight, out_bias[None]
    )
    score, first, first_b, second, second_b, out_w, out_b = write_results(score_and_gradient(
        latent.reshape(lat_rows, lon_cols, features), weights,
        jnp.transpose(truth, (1, 2, 0)), node_weight, members, bands, cols, rows, extra,
    ))
    return (score, first, first_b[0], second, second_b[0], out_w, out_b[0])


def solution(mesh):
    in_specs = (
        P("mem", "band", None, None),
        P(None, "band", "mem"),
        P("band", "mem"),
        P(),
        P(),
        P(),
        P(),
        P(),
        P(),
    )
    out_specs = (P("band", "mem"), P("mem", None), P(), P("mem", None), P(), P(), P())
    return jax.shard_map(body, mesh=mesh, in_specs=in_specs, out_specs=out_specs, check_vma=False)
```

```python
import functools
import math
import jax
import jax.numpy as jnp
from jax import lax
from jax.experimental import pallas as pl
from jax.experimental.pallas import tpu as pltpu
from jax.sharding import PartitionSpec as P

RADIUS = 3
LANES = 128
MESH = pl.DeviceIdType.MESH

root_half = 0.7071067811865476
density_scale = 0.3989422804014327
tap_spread = 1.5
epsilon = 1e-06


def gelu_pair(value):
    normal_cdf = 0.5 * (1.0 + lax.erf(value * root_half))
    return (value * normal_cdf, normal_cdf + value * jnp.exp(-0.5 * value * value) * density_scale)


def stencil_taps(radius):
    weights = [math.exp(-k * k / (2.0 * tap_spread * tap_spread)) for k in range(-radius, radius + 1)]
    return [w / sum(weights) for w in weights]


def remote(src, dst, send, recv, where):
    return pltpu.make_async_remote_copy(
        src_ref=src, dst_ref=dst, send_sem=send, recv_sem=recv, device_id=where, device_id_type=MESH
    )


def peer(me, p, count):
    if count & (count - 1):
        return lax.rem(me + p, count)
    total, bit = 0, 1
    while bit < count:
        total = total + lax.rem(me // bit + p // bit, 2) * bit
        bit *= 2
    return total


def smooth_block(before, own, after, taps, cols):
    edge, length = before.shape[1], own.shape[1]
    padded = jnp.concatenate([before, own, after], axis=1)
    width = padded.shape[1]
    rolled = {0: padded}
    total = None
    for index, tap in enumerate(taps):
        shift = (index - RADIUS) * cols
        rest = shift % LANES
        if rest not in rolled:
            rolled[rest] = pltpu.roll(padded, width - rest, 1)
        start = edge + shift - rest
        term = tap * rolled[rest][:, start : start + length]
        total = term if total is None else total + term
    return total


def contract(left, right, left_dim, right_dim):
    return lax.dot_general(
        left, right, (((left_dim,), (right_dim,)), ((), ())), preferred_element_type=jnp.float32
    )


def reduce_in_kernel(
    members, bands, first_sum, second_sum, small_sum, first_out, second_out, small_all,
    core_in, held, y_in, y_sum, x_wide, x_sum, x_in, y_late, pair, z_in, gather_w,
    t_core, t_held, t_y, t_ysum, t_x, t_xsum, t_z, final_s, gather_s, gather_b,
    sc, rc, sy, ry, sx, rx, sxw, rxw, syl, ryl, sz, rz, st, rt, stz, rtz, stg, rtg, sgw, rgw, sgb, rgb,
):
    me = lax.axis_index("mem")
    band = lax.axis_index("band")
    low, high = lax.rem(band, 2), band // 2
    parity, group = lax.rem(me, 2), me // 2
    groups = members // 2
    rows = first_out.shape[0]
    hidden = first_sum.shape[1]
    half, part = hidden // 2, hidden // bands
    extra = final_s.shape[0]
    partner = {"band": high * 2 + 1 - low}
    across = {"band": (1 - high) * 2 + low}
    beside = {"mem": me + 1 - 2 * parity}

    def cut(index, size):
        return pl.ds(pl.multiple_of(index * size, size), size)

    mine, other = cut(high, part), cut(1 - high, part)

    def both(q):
        return cut(q, 2 * rows)

    def kept(q):
        return cut(2 * q + parity, rows)

    def given(q):
        return cut(2 * q + 1 - parity, rows)

    def core(w, q):
        source = (second_sum, first_sum)[w]
        return remote(
            source.at[both(q), cut(1 - low, half)], core_in.at[w, both(q)], sc.at[w, q], rc.at[w, q], partner
        )

    def along_y(q):
        return remote(held.at[0, both(q), other], y_in.at[both(q)], sy.at[q], ry.at[q], across)

    def along_x(q):
        return remote(y_sum.at[given(q)], x_in.at[q], sx.at[q], rx.at[q], beside)

    def wide_x(q):
        return remote(held.at[1, given(q)], x_wide.at[q], sxw.at[q], rxw.at[q], beside)

    def late_y(q):
        return remote(x_sum.at[q, :, other], y_late.at[q], syl.at[q], ryl.at[q], across)

    def along_z(q):
        return remote(pair.at[q], z_in.at[group], sz.at[q], rz.at[group], {"mem": 2 * q + parity})

    small_core = remote(small_sum.at[:, cut(1 - low, half)], t_core, st.at[0], rt.at[0], partner)
    small_y = remote(t_held.at[:, other], t_y, st.at[1], rt.at[1], across)
    spread = groups * extra
    small_x = remote(t_ysum.at[cut(1 - parity, spread)], t_x, st.at[2], rt.at[2], beside)
    slot = parity * groups + group

    def small_z(q):
        return remote(t_xsum.at[cut(q, extra)], t_z.at[group], stz.at[q], rtz.at[group], {"mem": 2 * q + parity})

    def slot_of(k):
        return lax.rem(k, 2) * groups + k // 2

    def small_gather(k):
        return remote(final_s, gather_s.at[slot], stg.at[k], rtg.at[me], {"mem": k})

    def step_core(t, carry):
        q = peer(group, groups - 1 - t, groups)
        core(0, q).start()
        core(1, q).start()
        return carry

    small_core.start()
    lax.fori_loop(0, groups, step_core, 0)
    small_core.wait_recv()
    t_held[...] = small_sum[:, cut(low, half)] + t_core[...]
    small_y.start()

    def near(index):
        return peer(group, groups - 1 - index, groups)

    def step(t, carry):
        @pl.when(t < groups)
        def _():
            q = near(t)
            core(0, q).wait_recv()
            held[0, both(q)] = second_sum[both(q), cut(low, half)] + core_in[0, both(q)]
            along_y(q).start()
            core(1, q).wait_recv()
            held[1, both(q)] = first_sum[both(q), cut(low, half)] + core_in[1, both(q)]
            wide_x(q).start()

        @pl.when(t == 2)
        def _():
            small_y.wait_recv()
            t_ysum[...] = t_held[:, mine] + t_y[...]
            small_x.start()

        @pl.when((t >= 2) & (t < groups + 2))
        def _():
            q = near(t - 2)
            along_y(q).wait_recv()
            y_sum[both(q)] = held[0, both(q), mine] + y_in[both(q)]
            along_x(q).start()
            wide_x(q).wait_recv()
            x_sum[q] = held[1, kept(q)] + x_wide[q]
            late_y(q).start()

        @pl.when(t == 3)
        def _():
            small_x.wait_recv()
            t_xsum[...] = t_ysum[cut(parity, spread)] + t_x[...]

            def send(p, inner):
                small_z(peer(group, groups - p, groups)).start()
                return inner

            lax.fori_loop(1, groups, send, 0)

        @pl.when((t >= 4) & (t < groups + 4))
        def _():
            q = near(t - 4)
            along_x(q).wait_recv()
            pair[q, rows:] = y_sum[kept(q)] + x_in[q]
            late_y(q).wait_recv()
            pair[q, :rows] = x_sum[q, :, mine] + y_late[q]

            @pl.when(q != group)
            def _():
                along_z(q).start()

        @pl.when(t == 4)
        def _():
            def take(p, total):
                q = peer(group, p, groups)
                remote(t_z.at[q], t_z.at[q], stz.at[q], rtz.at[q], {"mem": 2 * q + parity}).wait_recv()
                return total + t_z[q]

            final_s[...] = lax.fori_loop(1, groups, take, t_xsum[cut(group, extra)])
            gather_s[slot] = final_s[...]

            def send(p, inner):
                small_gather(peer(me, members - p, members)).start()
                return inner

            lax.fori_loop(1, members, send, 0)

        return carry

    lax.fori_loop(0, max(groups, 4) + 4, step, 0)

    def weights(at, who, where):
        return remote(gather_w.at[at], gather_w.at[at], sgw.at[who], rgw.at[at], where)

    def smalls(at, who, where):
        return remote(gather_b.at[at], gather_b.at[at], sgb.at[who], rgb.at[at], where)

    far = (1 - high) * 2 + low
    near_by = high * 2 + 1 - low
    near_far = (1 - high) * 2 + 1 - low

    def take_small(p, carry):
        k = peer(me, p, members)
        at = slot_of(k)
        remote(gather_s.at[at], gather_s.at[at], stg.at[k], rtg.at[k], {"mem": k}).wait_recv()
        return carry

    lax.fori_loop(1, members, take_small, 0)
    gather_b[band] = gather_s[...]
    smalls(band, 0, across).start()
    smalls(band, 1, partner).start()

    def take_z(p, total):
        q = peer(group, groups - p, groups)
        remote(z_in.at[q], z_in.at[q], sz.at[q], rz.at[q], {"mem": 2 * q + parity}).wait_recv()
        return total + z_in[q]

    gather_w[band] = lax.fori_loop(1, groups, take_z, pair[group])
    weights(band, 0, across).start()
    weights(band, 1, partner).start()
    smalls(far, 2, across).wait_recv()
    smalls(far, 2, partner).start()
    weights(far, 2, across).wait_recv()
    weights(far, 2, partner).start()
    for at in (near_by, near_far):
        smalls(at, 0, partner).wait_recv()
        weights(at, 0, partner).wait_recv()
    for k in range(bands):
        lanes = slice((k % 2) * half + (k // 2) * part, (k % 2) * half + (k // 2) * part + part)
        first_out[:, lanes] = gather_w[k, :rows]
        second_out[:, lanes] = gather_w[k, rows:]
        small_all[:, lanes] = gather_b[k].reshape(small_all.shape[0], part)
    for at, who, where in ((band, 0, across), (band, 1, partner), (far, 2, partner)):
        weights(at, who, where).wait_send()
        smalls(at, who, where).wait_send()
    small_core.wait_send()
    small_y.wait_send()
    small_x.wait_send()

    def drain(k, carry):
        @pl.when(k != me)
        def _():
            small_gather(k).wait_send()

        return carry

    def drain_groups(q, carry):
        core(0, q).wait_send()
        core(1, q).wait_send()
        along_y(q).wait_send()
        along_x(q).wait_send()
        wide_x(q).wait_send()
        late_y(q).wait_send()

        @pl.when(q != group)
        def _():
            along_z(q).wait_send()
            small_z(q).wait_send()

        return carry

    lax.fori_loop(0, members, drain, 0)
    lax.fori_loop(0, groups, drain_groups, 0)


def reduce_scratch(members, bands, features, hidden, extra):
    groups, rows, half, part = members // 2, features // members, hidden // 2, hidden // bands
    dma = pltpu.SemaphoreType.DMA
    height = members * extra
    shapes = [
        (2, features, half), (2, features, half), (features, part), (features, part),
        (groups, rows, half), (groups, rows, half), (groups, rows, part), (groups, rows, part),
        (groups, 2 * rows, part), (groups, 2 * rows, part), (bands, 2 * rows, part),
        (height, half), (height, half), (height, part), (height, part),
        (height // 2, part), (height // 2, part), (groups, extra, part),
        (extra, part), (members, extra, part), (bands, members, extra, part),
    ]
    counts = (
        [(2, groups)] * 2 + [(groups,)] * 10 + [(3,)] * 2 + [(groups,)] * 2 + [(members,)] * 2 + [(bands,)] * 4
    )
    return [pltpu.VMEM(o, jnp.float32) for o in shapes] + [dma(n) for n in counts]


def score_kernel(
    members, bands, chunks, cols, edge,
    latent_ref, first_hbm, first_bias_hbm, second_hbm, second_bias_hbm, out_weight_hbm, out_bias_hbm,
    truth_hbm, node_hbm,
    score_out, first_out, first_bias_out, second_out, second_bias_out, out_weight_out, out_bias_out,
    first_ref, first_bias_ref, second_ref, second_bias_ref, out_weight_ref, out_bias_ref, truth_in, node_ref, inputs_sem,
    rows_in, first_act, first_slope, second_act, second_slope, first_sum, second_sum, small_sum, bias_sum, raw_ref,
    before, after, grad_before, grad_after, sent, ensemble, grads, returned, back,
    halo_send, halo_recv, ghalo_send, ghalo_recv, fwd_send, fwd_recv, ret_send, ret_recv, load,
    score_ref, weight_ref, truth_ref, bias_column, small_all, *reduce_refs,
):
    me = lax.axis_index("mem")
    band = lax.axis_index("band")
    length = raw_ref.shape[2]
    lat_rows = node_ref.shape[0]
    blocks = chunks * members
    taps = stencil_taps(RADIUS)
    has_prev = band > 0
    has_next = band < bands - 1
    prev, following = jnp.maximum(band - 1, 0), jnp.minimum(band + 1, bands - 1)

    def outward(s):
        p = lax.rem(s, members)
        far = members - 1 - p // 2
        return peer(me, jnp.where(lax.rem(p, 2) == 0, far, far - members // 2), members)

    def inward(s):
        return outward(lax.rem(s, members) + members - 1)

    def block_of(s, k):
        return (s // members) * members + k

    def fetch(s):
        chunk, k = s // members, outward(s)
        where = pl.ds(pl.multiple_of((k * chunks + chunk) * cols, cols), cols)
        b = block_of(s, k)
        return pltpu.make_async_copy(latent_ref.at[:, where, :], rows_in.at[b], load.at[b])

    def prefetch(s, carry):
        fetch(s).start()
        return carry

    barrier = pltpu.get_barrier_semaphore()

    def greet(p, carry):
        pl.semaphore_signal(barrier, inc=1, device_id={"mem": peer(me, members - p, members)}, device_id_type=MESH)
        return carry

    lax.fori_loop(1, members, greet, 0)

    for d in range(1, bands):
        pl.semaphore_signal(barrier, inc=1, device_id={"band": lax.rem(band + d, bands)}, device_id_type=MESH)

    pairs = (
        (first_hbm, first_ref), (first_bias_hbm, first_bias_ref), (second_hbm, second_ref),
        (second_bias_hbm, second_bias_ref), (out_weight_hbm, out_weight_ref), (out_bias_hbm, out_bias_ref),
        (truth_hbm, truth_in), (node_hbm, node_ref),
    )
    loads = [pltpu.make_async_copy(source, target, inputs_sem.at[i]) for i, (source, target) in enumerate(pairs)]
    for copy in loads[:2]:
        copy.start()
    fetch(0).start()
    for copy in loads[2:6]:
        copy.start()
    lax.fori_loop(1, blocks, prefetch, 0)
    for copy in loads[6:]:
        copy.start()
    channels, hidden = out_weight_ref.shape
    @pl.when(band == 0)
    def _():
        before[...] = jnp.zeros_like(before)
        grad_before[...] = jnp.zeros_like(grad_before)

    @pl.when(band == bands - 1)
    def _():
        after[...] = jnp.zeros_like(after)
        grad_after[...] = jnp.zeros_like(grad_after)

    def to_next(source, target, b, send, recv):
        return remote(source.at[b, :, pl.ds(length - edge, edge)], target.at[b], send.at[0, b], recv.at[0, b], {"band": following})

    def to_prev(source, target, b, send, recv):
        return remote(source.at[b, :, pl.ds(0, edge)], target.at[b], send.at[1, b], recv.at[1, b], {"band": prev})

    def start_edges(source, low, high, b, send, recv):
        @pl.when(has_next)
        def _():
            to_next(source, low, b, send, recv).start()

        @pl.when(has_prev)
        def _():
            to_prev(source, high, b, send, recv).start()

    def wait_edges(source, low, high, b, send, recv):
        @pl.when(has_prev)
        def _():
            to_next(source, low, b, send, recv).wait_recv()

        @pl.when(has_next)
        def _():
            to_prev(source, high, b, send, recv).wait_recv()

    def drain_edges(source, low, high, b, send, recv):
        @pl.when(has_next)
        def _():
            to_next(source, low, b, send, recv).wait_send()

        @pl.when(has_prev)
        def _():
            to_prev(source, high, b, send, recv).wait_send()

    raw_edges = (raw_ref, before, after)
    grad_edges = (grads, grad_before, grad_after)

    def forward(s, k):
        b = block_of(s, k)
        return remote(sent.at[b], ensemble.at[block_of(s, me)], fwd_send.at[b], fwd_recv.at[block_of(s, me)], {"mem": k})

    def returning(s, k):
        b = block_of(s, k)
        return remote(returned.at[b], back.at[block_of(s, me)], ret_send.at[b], ret_recv.at[block_of(s, me)], {"mem": k})

    def arrived(buffer, sems, s, k):
        b = block_of(s, k)
        remote(buffer.at[b], buffer.at[b], sems.at[b], sems.at[b], {"mem": k}).wait_recv()

    def decode(s):
        b = block_of(s, outward(s))
        fetch(s).wait()
        inputs = rows_in[b].reshape(length, rows_in.shape[3])
        pre = jnp.dot(inputs, first_ref[...], preferred_element_type=jnp.float32) + first_bias_ref[...]
        act, slope = gelu_pair(pre)
        first_act[b] = act.astype(jnp.bfloat16)
        first_slope[b] = slope
        pre = jnp.dot(first_act[b], second_ref[...], preferred_element_type=jnp.float32) + second_bias_ref[...]
        act, slope = gelu_pair(pre)
        second_act[b] = act.astype(jnp.bfloat16)
        second_slope[b] = slope
        raw_ref[b] = contract(out_weight_ref[...], second_act[b], 1, 1) + bias_column[...]

    def decode_edges(s):
        start_edges(*raw_edges, block_of(s, outward(s)), halo_send, halo_recv)

    def spread(s):
        k = outward(s)
        b = block_of(s, k)
        wait_edges(*raw_edges, b, halo_send, halo_recv)
        smooth = smooth_block(before[b], raw_ref[b], after[b], taps, cols)

        @pl.when(k != me)
        def _():
            sent[b] = smooth
            forward(s, k).start()

        @pl.when(k == me)
        def _():
            ensemble[b] = smooth

    lead = 2

    def early_step(s, carry):
        decode(s)
        return carry

    def early_edges(s, carry):
        decode_edges(s)
        return carry

    def forward_step(s, carry):
        @pl.when(s < blocks)
        def _():
            decode(s)
            decode_edges(s)

        spread(s - lead)
        return carry

    for copy in loads[:6]:
        copy.wait()
    shape = (channels, channels)
    diagonal = lax.broadcasted_iota(jnp.int32, shape, 0) == lax.broadcasted_iota(jnp.int32, shape, 1)
    bias_column[...] = jnp.sum(jnp.where(diagonal, out_bias_ref[...], 0.0), axis=1, keepdims=True)
    lax.fori_loop(0, lead, early_step, 0)
    pl.semaphore_wait(barrier, members + bands - 2)
    lax.fori_loop(0, lead, early_edges, 0)
    lax.fori_loop(lead, blocks + lead, forward_step, 0)
    for copy in loads[6:]:
        copy.wait()
    for c in range(chunks):
        truth_ref[c] = truth_in[:, c * cols : (c + 1) * cols, :].reshape(length, channels).T
        for row in range(lat_rows):
            weight_ref[c, :, row * cols : (row + 1) * cols] = node_ref[row : row + 1, c * cols : (c + 1) * cols]
    first_sum[...] = jnp.zeros_like(first_sum)
    second_sum[...] = jnp.zeros_like(second_sum)
    small_sum[...] = jnp.zeros_like(small_sum)
    bias_sum[...] = jnp.zeros_like(bias_sum)
    score_ref[...] = jnp.zeros_like(score_ref)
    pair_count = members * (members - 1)
    row_ids = lax.broadcasted_iota(jnp.int32, (members, LANES), 0)

    def score_chunk(c, carry):
        start = c * members

        def collect(p, inner):
            arrived(ensemble, fwd_recv, start, peer(me, p, members))
            return inner

        lax.fori_loop(1, members, collect, 0)

        def member(p, inner):
            m = outward(p)
            b = start + m

            def piece(i, innermost):
                lanes = pl.ds(pl.multiple_of(i * LANES, LANES), LANES)
                mine = ensemble[b, :, lanes]
                gaps = mine[None] - ensemble[pl.ds(start, members), :, lanes]
                distance = jnp.sqrt(jnp.sum(gaps * gaps, axis=1) + epsilon)
                own = row_ids == m
                inverse = jnp.where(own, 0.0, 1.0 / distance)
                spread_sum = jnp.sum(jnp.where(own, 0.0, distance), axis=0, keepdims=True)
                pair_grad = jnp.sum(gaps * inverse[:, None, :], axis=0)
                error = mine - truth_ref[c, :, lanes]
                skill = jnp.sqrt(jnp.sum(error * error, axis=0, keepdims=True) + epsilon)
                score_ref[c, :, lanes] += skill / members - spread_sum / (2.0 * pair_count)
                grads[b, :, lanes] = weight_ref[c, :, lanes] * (error / (members * skill) - pair_grad / pair_count)
                return innermost

            lax.fori_loop(0, length // LANES, piece, 0)
            start_edges(*grad_edges, b, ghalo_send, ghalo_recv)
            return inner

        lax.fori_loop(0, members, member, 0)

        def give(p, inner):
            m = outward(p)
            b = start + m
            wait_edges(*grad_edges, b, ghalo_send, ghalo_recv)
            smooth = smooth_block(grad_before[b], grads[b], grad_after[b], taps, cols)

            @pl.when(m != me)
            def _():
                returned[b] = smooth
                returning(start, m).start()

            @pl.when(m == me)
            def _():
                back[b] = smooth

            return inner

        lax.fori_loop(0, members, give, 0)
        return carry

    lax.fori_loop(0, chunks, score_chunk, 0)

    def finish(s, carry):
        k = inward(s)
        b = block_of(s, k)

        @pl.when(k != me)
        def _():
            arrived(back, ret_recv, s, k)

        grad_raw = back[b]
        grad_low = grad_raw.astype(jnp.bfloat16)
        bias_sum[...] += jnp.sum(grad_raw, axis=1, keepdims=True)
        small_sum[:channels] += jnp.dot(grad_low, second_act[b], preferred_element_type=jnp.float32)
        delta = contract(grad_low, out_weight_ref[...], 0, 0) * second_slope[b]
        small_sum[channels + 1 : channels + 2] += jnp.sum(delta, axis=0, keepdims=True)
        low = delta.astype(jnp.bfloat16)
        second_sum[...] += contract(first_act[b], low, 0, 0)
        delta = contract(low, second_ref[...], 1, 1) * first_slope[b]
        small_sum[channels : channels + 1] += jnp.sum(delta, axis=0, keepdims=True)
        inputs = rows_in[b].reshape(length, rows_in.shape[3])
        first_sum[...] += contract(inputs, delta.astype(jnp.bfloat16), 0, 0)
        return carry

    lax.fori_loop(0, blocks, finish, 0)
    small_sum[channels + 2 : channels + 3, :channels] = jnp.sum(
        jnp.where(diagonal, bias_sum[...], 0.0), axis=0, keepdims=True
    )
    reduce_in_kernel(
        members, bands, first_sum, second_sum, small_sum, first_out, second_out, small_all, *reduce_refs
    )
    for c in range(chunks):
        for row in range(lat_rows):
            score_out[row : row + 1, c * cols : (c + 1) * cols] = score_ref[c, :, row * cols : (row + 1) * cols]
    out_weight_out[...] = small_all[:channels]
    first_bias_out[...] = small_all[channels : channels + 1]
    second_bias_out[...] = small_all[channels + 1 : channels + 2]
    out_bias_out[...] = small_all[channels + 2 : channels + 3, :channels]

    def drain(s, carry):
        k = inward(s)
        b = block_of(s, k)
        drain_edges(*raw_edges, b, halo_send, halo_recv)
        drain_edges(*grad_edges, b, ghalo_send, ghalo_recv)

        @pl.when(k != me)
        def _():
            forward(s, k).wait_send()
            returning(s, k).wait_send()

        return carry

    lax.fori_loop(0, blocks, drain, 0)


def score_and_gradient(latent, weights, truth, weight, members, bands, cols, rows, extra):
    lat_rows, _, features = latent.shape
    channels = truth.shape[2]
    hidden = weights[0].shape[1]
    chunks = 2 if cols % 32 == 0 and lat_rows * cols % (2 * LANES) == 0 else 1
    part_cols = cols // chunks
    length = lat_rows * part_cols
    edge = min(length, -(-RADIUS * part_cols // LANES) * LANES)
    blocks = chunks * members
    block = (blocks, channels, length)
    halo = (blocks, channels, edge)
    units = (blocks, length, hidden)
    dma = pltpu.SemaphoreType.DMA
    vmem = pl.BlockSpec(memory_space=pltpu.VMEM)
    single, half = jnp.float32, jnp.bfloat16
    return pl.pallas_call(
        functools.partial(score_kernel, members, bands, chunks, part_cols, edge),
        out_shape=tuple(
            pltpu.VMEM(o, single)
            for o in (
                (lat_rows, cols), (rows, hidden), (1, hidden), (rows, hidden), (1, hidden),
                (channels, hidden), (1, channels),
            )
        ),
        in_specs=[pl.BlockSpec(memory_space=pl.ANY)] * 9,
        out_specs=(vmem,) * 7,
        scratch_shapes=[pltpu.VMEM(v.shape, v.dtype) for v in (*weights, truth, weight)]
        + [dma((8,))]
        + [
            pltpu.VMEM((blocks, lat_rows, part_cols, features), half),
            pltpu.VMEM(units, half), pltpu.VMEM(units, single),
            pltpu.VMEM(units, half), pltpu.VMEM(units, single),
            pltpu.VMEM((features, hidden), single), pltpu.VMEM((hidden, hidden), single),
            pltpu.VMEM((members * extra, hidden), single), pltpu.VMEM((channels, 1), single),
            pltpu.VMEM(block, single),
        ]
        + [pltpu.VMEM(halo, single)] * 4
        + [pltpu.VMEM(block, single)] * 5
        + [dma((2, blocks))] * 4
        + [dma((blocks,))] * 5
        + [pltpu.VMEM(o, single) for o in [
            (chunks, 1, length), (chunks, 1, length), (chunks, channels, length), (channels, 1),
            (members * extra, hidden),
        ]]
        + reduce_scratch(members, bands, features, hidden, extra),
        compiler_params=pltpu.CompilerParams(collective_id=0, has_side_effects=True, vmem_limit_bytes=58 << 20),
    )(latent, *weights, truth, weight)


def write_kernel(*refs):
    count = len(refs) // 2
    for source, target in zip(refs[:count], refs[count:]):
        target[...] = source[...]


def write_results(values):
    vmem = pl.BlockSpec(memory_space=pltpu.VMEM)
    values = [pltpu.with_memory_space_constraint(v, pltpu.VMEM) for v in values]
    return pl.pallas_call(
        write_kernel,
        out_shape=tuple(jax.ShapeDtypeStruct(v.shape, v.dtype) for v in values),
        in_specs=[vmem] * len(values),
        out_specs=(vmem,) * len(values),
    )(*values)


def body(
    latent, truth, node_weight, first_weight, first_bias, second_weight, second_bias, out_weight, out_bias
):
    members, bands = lax.axis_size("mem"), lax.axis_size("band")
    _, lat_rows, lon_cols, features = latent.shape
    channels, hidden = out_weight.shape
    cols = lon_cols // members
    rows = features // members
    extra = -(-(channels + 3) // (8 * members)) * 8
    weights = (
        first_weight, first_bias[None], second_weight, second_bias[None], out_weight, out_bias[None]
    )
    score, first, first_b, second, second_b, out_w, out_b = write_results(score_and_gradient(
        latent.reshape(lat_rows, lon_cols, features), weights,
        jnp.transpose(truth, (1, 2, 0)), node_weight, members, bands, cols, rows, extra,
    ))
    return (score, first, first_b[0], second, second_b[0], out_w, out_b[0])


def solution(mesh):
    in_specs = (
        P("mem", "band", None, None),
        P(None, "band", "mem"),
        P("band", "mem"),
        P(),
        P(),
        P(),
        P(),
        P(),
        P(),
    )
    out_specs = (P("band", "mem"), P("mem", None), P(), P("mem", None), P(), P(), P())
    return jax.shard_map(body, mesh=mesh, in_specs=in_specs, out_specs=out_specs, check_vma=False)
```
